256 devices in a mesh: wl: 16 (over y, x), cell: 16 (over z, core).
Axes of the slice: x: 4, y: 4, z: 8, core: 2. Of those that a mesh axis runs over, the one named last changes fastest.
Arguments:
- interfaces: float32 [8, 3, 2, 128, 128], replicated, may hold values from -0.10606602 to 1.006066
- cell_profile: int32 [128], P('cell'), may hold values from 0 to 3
- cell_section: int32 [128], P('cell'), may hold values from 0 to 7
- mode_loss: float32 [4, 128], replicated, may hold values from 0.985 to 1
- phase: float32 [4, 16, 128], P(None, 'wl'), may hold values from -3.140625 to 3.140625
- mode_field: float32 [4, 128, 4096], P(None, None, 'wl'), may hold values from -0.5 to 0.5
- target: float32 [16, 2, 128, 128], P('wl'), may hold values from -0.5 to 0.5
Outputs:
- reflection: float32 [16, 2, 128, 128], P('wl', None, 'cell')
- gradient: float32 [128, 4096], P('cell', 'wl')
The draws below stay inside these ranges and needn't reach their ends.
All inputs are finite; a program needn't handle non-finite values.
Results may differ from the reference program's by a relative error of at most 0.0003.
Values sent between devices are 32-bit elements; how exact they have to be, the bound alone decides.
A program may use at most 128 MiB of HBM per device.

```python
import math
import jax
import jax.numpy as jnp
from jax import lax

MODES = 128
PIXELS = 4096
PROFILES = 4
SECTIONS = 8
CELLS = 128
WAVES = 16


def draw_interfaces(key, part):
    full_shape = (SECTIONS, 3, 2, MODES, MODES)
    unit_matrix = jnp.eye(MODES, dtype=jnp.float32)
    random_part = jnp.clip(jax.random.normal(key, full_shape, jnp.float32), -4.0, 4.0)
    spread_value = 0.3
    center = 0.9
    kind_scale = jnp.array([0.7, 1.0, 1.0], jnp.float32) * (spread_value / MODES ** 0.5)
    values = random_part * kind_scale[None, :, None, None, None]
    kind_mask = jnp.array([0.0, 1.0, 1.0], jnp.float32)[None, :, None, None, None]
    part_mask = jnp.array([1.0, 0.0], jnp.float32)[None, None, :, None, None]
    return values + kind_mask * part_mask * center * unit_matrix


def plant(drawn, own_key, smallest, top_value):
    longest = drawn.shape.index(max(drawn.shape))
    spots = []
    for shift in (0, 1):
        where = [jax.random.randint(jax.random.fold_in(own_key, axis), (), 0, length) for axis, length in enumerate(drawn.shape)]
        where[longest] = (where[longest] + shift) % drawn.shape[longest]
        spots.append(tuple(where))
    return drawn.at[spots[0]].set(smallest).at[spots[1]].set(top_value)


def block_scale(key, shape, shards, low, top_value):
    def one(axis_at, blocks):
        heights = jax.random.uniform(jax.random.fold_in(jax.random.fold_in(key, 6), axis_at), (blocks,), jnp.float32, low / len(shards), top_value / len(shards))
        return jnp.repeat(jnp.exp(heights), shape[axis_at] // blocks).reshape((-1,) + (1,) * (len(shape) - axis_at - 1))

    level = one(*shards[0])
    for cut in shards[1:]:
        level = level * one(*cut)
    return level


def normal_values(rng, dims, width, reach, shards=(), kind=jnp.bfloat16):
    entries = width * jax.random.normal(rng, dims, jnp.float32)
    if shards:
        entries = entries * block_scale(rng, dims, shards, -0.22, 0.18)
    return jnp.clip(entries, -reach, reach).astype(kind)


def setup_inputs(seed: int = 0) -> dict:
    streams_of = jax.random.split(jax.random.key(seed), 8)
    return {
        "interfaces": draw_interfaces(jax.random.fold_in(streams_of[7], 71), 0),
        "cell_profile": plant(jax.random.randint(streams_of[1], (CELLS,), 0, PROFILES), jax.random.fold_in(streams_of[1], 1), 0, PROFILES - 1).astype(jnp.int32),
        "cell_section": plant(jax.random.randint(streams_of[2], (CELLS,), 0, SECTIONS), jax.random.fold_in(streams_of[2], 1), 0, SECTIONS - 1).astype(jnp.int32),
        "mode_loss": jnp.clip(jnp.exp(jax.random.uniform(streams_of[3], (PROFILES, MODES), jnp.float32, math.log(0.985), math.log(1.0))), 0.985, 1.0),
        "phase": jnp.clip(jax.random.uniform(streams_of[4], (PROFILES, WAVES, MODES), jnp.float32, -3.140625, 3.140625), -3.140625, 3.140625),
        "mode_field": normal_values(streams_of[5], (PROFILES, MODES, PIXELS), MODES ** -0.5, 0.5, ((2, 16),), jnp.float32),
        "target": normal_values(streams_of[6], (WAVES, 2, MODES, MODES), MODES ** -0.5, 0.5, ((0, 16),), jnp.float32),
    }


def matmul_highest(first, second):
    return jnp.matmul(first, second, precision=lax.Precision.HIGHEST)


def complex_product(left_matrix, right_matrix):
    left_real = left_matrix[..., 0, :, :]
    left_imag = left_matrix[..., 1, :, :]
    right_real = right_matrix[..., 0, :, :]
    right_imag = right_matrix[..., 1, :, :]
    real_part = matmul_highest(left_real, right_real) - matmul_highest(left_imag, right_imag)
    imag_part = matmul_highest(left_real, right_imag) + matmul_highest(left_imag, right_real)
    return jnp.stack([real_part, imag_part], axis=-3)


def star_product(former, latter):
    refl_former, trans_former, back_former = former
    refl_latter, trans_latter, back_latter = latter
    reflect = refl_former + complex_product(complex_product(back_former, refl_latter), trans_former)
    return (reflect, complex_product(trans_latter, trans_former), complex_product(back_former, back_latter))


def transpose_complex(matrix):
    return jnp.swapaxes(matrix, -1, -2)


def build_cells(selected, prop_real, prop_imag):
    forward = selected[..., 1, :, :, :]
    backward = selected[..., 2, :, :, :]
    row_real = prop_real[..., :, None]
    row_imag = prop_imag[..., :, None]
    trans = jnp.stack([row_real * forward[..., 0, :, :] - row_imag * forward[..., 1, :, :],
                       row_real * forward[..., 1, :, :] + row_imag * forward[..., 0, :, :]], axis=-3)
    col_real = prop_real[..., None, :]
    col_imag = prop_imag[..., None, :]
    back = jnp.stack([backward[..., 0, :, :] * col_real - backward[..., 1, :, :] * col_imag,
                      backward[..., 0, :, :] * col_imag + backward[..., 1, :, :] * col_real], axis=-3)
    reflect = jnp.broadcast_to(selected[..., 0, :, :, :], trans.shape)
    return (reflect, trans, back)


def reference(interfaces, cell_profile, cell_section, mode_loss, phase, mode_field, target):
    cell_count = cell_profile.shape[0]
    mode_count = mode_loss.shape[1]
    wave_count = phase.shape[1]
    group_size = math.gcd(wave_count, 8)
    selected = interfaces[cell_section]
    amplitude = mode_loss[cell_profile]
    unit_matrix = jnp.stack([jnp.eye(mode_count, dtype=jnp.float32),
                             jnp.zeros((mode_count, mode_count), jnp.float32)])
    identity = jnp.broadcast_to(unit_matrix, (group_size, 2, mode_count, mode_count))
    zero_block = jnp.zeros_like(identity)
    phase_groups = jnp.moveaxis(phase, 1, 0).reshape(wave_count // group_size, group_size, phase.shape[0], mode_count)
    target_groups = target.reshape(wave_count // group_size, group_size, 2, mode_count, mode_count)

    def one_group(coupling, inputs):
        group_phase, group_target = inputs
        angle = jnp.moveaxis(group_phase[:, cell_profile], 1, 0)
        cells = build_cells(selected[:, None], amplitude[:, None, :] * jnp.cos(angle),
                            amplitude[:, None, :] * jnp.sin(angle))

        def forward_step(carry, trans):
            return complex_product(trans, carry), carry

        final_carry, prefix = lax.scan(forward_step, identity, cells[1])

        def backward_step(carry, cell):
            joined = star_product(cell, carry)
            return joined, joined

        last_carry, suffix = lax.scan(backward_step, (zero_block, identity, identity), cells, reverse=True)
        mismatch = suffix[1][0] - group_target
        fields = prefix + complex_product(suffix[0], prefix)
        adjoint = complex_product(transpose_complex(suffix[1]), mismatch)
        real_term = jnp.einsum("cwij,cwkj->cik", fields[:, :, 0], adjoint[:, :, 0], precision=lax.Precision.HIGHEST)
        imag_term = jnp.einsum("cwij,cwkj->cik", fields[:, :, 1], adjoint[:, :, 1], precision=lax.Precision.HIGHEST)
        return coupling + (real_term - imag_term), suffix[0][0]

    coupling, reflection = lax.scan(one_group, jnp.zeros((cell_count, mode_count, mode_count), jnp.float32),
                                    (phase_groups, target_groups))
    reflection = reflection.reshape(wave_count, 2, mode_count, mode_count)

    def project(inputs):
        cell_coupling, profile_index = inputs
        profile_field = mode_field[profile_index]
        return jnp.sum(profile_field * matmul_highest(cell_coupling, profile_field), axis=0)

    gradient = lax.map(project, (coupling, cell_profile))
    return reflection, gradient
```

```python
import jax
import jax.numpy as jnp
from jax import lax
from jax.sharding import PartitionSpec as P

HIGHEST = lax.Precision.HIGHEST


def cmul(left, right):
    parts = jnp.einsum("...pmk,...qkn->...pqmn", left, right, precision=HIGHEST)
    real = parts[..., 0, 0, :, :] - parts[..., 1, 1, :, :]
    imag = parts[..., 0, 1, :, :] + parts[..., 1, 0, :, :]
    return jnp.stack([real, imag], axis=-3)


def star(former, latter, need_back=True):
    refl_f, trans_f, back_f = former
    refl_l, trans_l, back_l = latter
    reflect = refl_f + cmul(cmul(back_f, refl_l), trans_f)
    trans = cmul(trans_l, trans_f)
    back = cmul(back_f, back_l) if need_back else None
    return (reflect, trans, back)


def pick(flag, a, b):
    return jax.tree.map(lambda u, v: jnp.where(flag, u, v), a, b)


def cat(a, b):
    return jax.tree.map(lambda u, v: jnp.concatenate([u, v], axis=0), a, b)


def suffix_scan(cells):
    count = cells[0].shape[0]
    shift = 1
    while shift < count:
        head = jax.tree.map(lambda a: a[: count - shift], cells)
        tail = jax.tree.map(lambda a: a[shift:], cells)
        joined = star(head, tail)
        cells = cat(joined, jax.tree.map(lambda a: a[count - shift :], cells))
        shift *= 2
    return cells


def prefix_scan(trans):
    count = trans.shape[0]
    shift = 1
    while shift < count:
        joined = cmul(trans[shift:], trans[: count - shift])
        trans = jnp.concatenate([trans[:shift], joined], axis=0)
        shift *= 2
    return trans


def build_cells(selected, prop_real, prop_imag):
    forward = selected[:, :, 1]
    backward = selected[:, :, 2]
    row_real = prop_real[..., :, None]
    row_imag = prop_imag[..., :, None]
    trans = jnp.stack(
        [
            row_real * forward[:, :, 0] - row_imag * forward[:, :, 1],
            row_real * forward[:, :, 1] + row_imag * forward[:, :, 0],
        ],
        axis=2,
    )
    col_real = prop_real[..., None, :]
    col_imag = prop_imag[..., None, :]
    back = jnp.stack(
        [
            backward[:, :, 0] * col_real - backward[:, :, 1] * col_imag,
            backward[:, :, 0] * col_imag + backward[:, :, 1] * col_real,
        ],
        axis=2,
    )
    reflect = jnp.broadcast_to(selected[:, :, 0], trans.shape)
    return (reflect, trans, back)


def body(interfaces, cell_profile, cell_section, mode_loss, phase, mode_field, target):
    mode_count = mode_loss.shape[1]
    waves_here = phase.shape[1]
    devices = lax.axis_size("cell")
    place = lax.axis_index("cell")

    selected = jnp.take(interfaces, cell_section, axis=0)[:, None]
    amplitude = jnp.take(mode_loss, cell_profile, axis=0)[:, None, :]
    angle = jnp.take(phase, cell_profile, axis=0)
    cells = build_cells(selected, amplitude * jnp.cos(angle), amplitude * jnp.sin(angle))

    unit = jnp.stack(
        [jnp.eye(mode_count, dtype=jnp.float32), jnp.zeros((mode_count, mode_count), jnp.float32)]
    )
    unit = jnp.broadcast_to(unit, (waves_here, 2, mode_count, mode_count))
    zero = jnp.zeros_like(unit)

    local_suffix = suffix_scan(cells)
    local_prefix = prefix_scan(cells[1])
    local_incoming = jnp.concatenate([unit[None], local_prefix[:-1]], axis=0)

    total = jax.tree.map(lambda a: a[0], local_suffix)
    right = (zero, unit, unit)
    left = unit
    shift = 1
    while shift < devices:
        last = shift * 2 >= devices
        perm = [(i, i ^ shift) for i in range(devices)]
        other = jax.tree.map(lambda a: lax.ppermute(a, "cell", perm), total)
        upper = (place & shift) == 0
        first = pick(upper, total, other)
        second = pick(upper, other, total)
        joined = star(
            jax.tree.map(lambda a, b: jnp.stack([a, b]), right, first),
            jax.tree.map(lambda a, b: jnp.stack([a, b]), other, second),
            need_back=not last,
        )
        right = tuple(
            None if n is None else jnp.where(upper, n[0], r) for n, r in zip(joined, right)
        )
        total = tuple(None if n is None else n[1] for n in joined)
        left = jnp.where(upper, left, cmul(left, other[1]))
        shift *= 2

    suffix_refl = local_suffix[0] + cmul(cmul(local_suffix[2], right[0][None]), local_suffix[1])
    suffix_trans = cmul(right[1][None], local_suffix[1])
    incoming = cmul(local_incoming, left[None])

    mismatch = total[1] - target
    fields = incoming + cmul(suffix_refl, incoming)
    adjoint = cmul(jnp.swapaxes(suffix_trans, -1, -2), mismatch[None])
    coupling = jnp.einsum(
        "cwij,cwkj->cik", fields[:, :, 0], adjoint[:, :, 0], precision=HIGHEST
    ) - jnp.einsum("cwij,cwkj->cik", fields[:, :, 1], adjoint[:, :, 1], precision=HIGHEST)
    summed = lax.psum(coupling, "wl")
    chosen = jnp.take(mode_field, cell_profile, axis=0)
    weighted = jnp.einsum("cmn,cnx->cmx", summed, chosen, precision=HIGHEST)
    gradient = jnp.sum(chosen * weighted, axis=1)

    row_count = mode_count // devices
    mine = lax.dynamic_slice_in_dim(total[0], place * row_count, row_count, 2)
    return (mine, gradient)


def solution(mesh):
    in_specs = (
        P(),
        P("cell"),
        P("cell"),
        P(),
        P(None, "wl", None),
        P(None, None, "wl"),
        P("wl", None, None, None),
    )
    out_specs = (P("wl", None, "cell", None), P("cell", "wl"))
    return jax.shard_map(body, mesh=mesh, in_specs=in_specs, out_specs=out_specs, check_vma=False)
```

```python
import functools

import jax
import jax.numpy as jnp
from jax import lax
from jax.experimental import pallas as pl
from jax.experimental.pallas import tpu as pltpu
from jax.sharding import PartitionSpec as P

HIGHEST = lax.Precision.HIGHEST


def cmul(left, right):
    parts = jnp.einsum("...pmk,...qkn->...pqmn", left, right, precision=HIGHEST)
    real = parts[..., 0, 0, :, :] - parts[..., 1, 1, :, :]
    imag = parts[..., 0, 1, :, :] + parts[..., 1, 0, :, :]
    return jnp.stack([real, imag], axis=-3)


def star(former, latter, need_back=True):
    refl_f, trans_f, back_f = former
    refl_l, trans_l, back_l = latter
    reflect = refl_f + cmul(cmul(back_f, refl_l), trans_f)
    trans = cmul(trans_l, trans_f)
    back = cmul(back_f, back_l) if need_back else None
    return (reflect, trans, back)


def pick(flag, a, b):
    return jax.tree.map(lambda u, v: jnp.where(flag, u, v), a, b)


def cat(a, b):
    return jax.tree.map(lambda u, v: jnp.concatenate([u, v], axis=0), a, b)


def suffix_scan(cells):
    count = cells[0].shape[0]
    shift = 1
    while shift < count:
        head = jax.tree.map(lambda a: a[: count - shift], cells)
        tail = jax.tree.map(lambda a: a[shift:], cells)
        joined = star(head, tail)
        cells = cat(joined, jax.tree.map(lambda a: a[count - shift :], cells))
        shift *= 2
    return cells


def prefix_scan(trans):
    count = trans.shape[0]
    shift = 1
    while shift < count:
        joined = cmul(trans[shift:], trans[: count - shift])
        trans = jnp.concatenate([trans[:shift], joined], axis=0)
        shift *= 2
    return trans


def build_cells(selected, prop_real, prop_imag):
    forward = selected[:, :, 1]
    backward = selected[:, :, 2]
    row_real = prop_real[..., :, None]
    row_imag = prop_imag[..., :, None]
    trans = jnp.stack(
        [
            row_real * forward[:, :, 0] - row_imag * forward[:, :, 1],
            row_real * forward[:, :, 1] + row_imag * forward[:, :, 0],
        ],
        axis=2,
    )
    col_real = prop_real[..., None, :]
    col_imag = prop_imag[..., None, :]
    back = jnp.stack(
        [
            backward[:, :, 0] * col_real - backward[:, :, 1] * col_imag,
            backward[:, :, 0] * col_imag + backward[:, :, 1] * col_real,
        ],
        axis=2,
    )
    reflect = jnp.broadcast_to(selected[:, :, 0], trans.shape)
    return (reflect, trans, back)


def wl_sum_kernel(count, part_ref, out_ref, held, send_a, recv_a, send_b, recv_b):
    me = lax.axis_index("wl")
    row = lax.axis_index("cell")
    mesh_id = pl.DeviceIdType.MESH

    def link(src, dst, send, recv, peer):
        return pltpu.make_async_remote_copy(
            src_ref=src, dst_ref=dst, send_sem=send, recv_sem=recv,
            device_id=(peer, row), device_id_type=mesh_id,
        )

    barrier = pltpu.get_barrier_semaphore()
    for step in range(1, count):
        peer = lax.rem(me + step, count)
        pl.semaphore_signal(barrier, inc=1, device_id=(peer, row), device_id_type=mesh_id)
    pl.semaphore_wait(barrier, count - 1)

    outgoing = []
    for step in range(1, count):
        peer = lax.rem(me + step, count)
        copy = link(part_ref.at[peer], held.at[me], send_a.at[peer], recv_a.at[me], peer)
        copy.start()
        outgoing.append(copy)
    total = part_ref[me]
    for step in range(1, count):
        source = lax.rem(me + count - step, count)
        link(part_ref.at[source], held.at[source], send_a.at[source], recv_a.at[source], source).wait_recv()
        total = total + held[source]
    out_ref[me] = total
    for copy in outgoing:
        copy.wait_send()

    outgoing = []
    for step in range(1, count):
        peer = lax.rem(me + step, count)
        copy = link(out_ref.at[me], out_ref.at[me], send_b.at[peer], recv_b.at[me], peer)
        copy.start()
        outgoing.append(copy)
    for step in range(1, count):
        source = lax.rem(me + count - step, count)
        link(out_ref.at[source], out_ref.at[source], send_b.at[source], recv_b.at[source], source).wait_recv()
    for copy in outgoing:
        copy.wait_send()


def wl_sum(value):
    count = lax.axis_size("wl")
    lanes = value.shape[-1]
    parts = value.reshape(count, -1, lanes)
    summed = pl.pallas_call(
        functools.partial(wl_sum_kernel, count),
        out_shape=jax.ShapeDtypeStruct(parts.shape, parts.dtype),
        in_specs=[pl.BlockSpec(memory_space=pltpu.VMEM)],
        out_specs=pl.BlockSpec(memory_space=pltpu.VMEM),
        scratch_shapes=[
            pltpu.VMEM(parts.shape, parts.dtype),
            pltpu.SemaphoreType.DMA((count,)),
            pltpu.SemaphoreType.DMA((count,)),
            pltpu.SemaphoreType.DMA((count,)),
            pltpu.SemaphoreType.DMA((count,)),
        ],
        compiler_params=pltpu.CompilerParams(collective_id=0, has_side_effects=True),
    )(parts)
    return summed.reshape(value.shape)


def body(interfaces, cell_profile, cell_section, mode_loss, phase, mode_field, target):
    mode_count = mode_loss.shape[1]
    waves_here = phase.shape[1]
    devices = lax.axis_size("cell")
    place = lax.axis_index("cell")

    selected = jnp.take(interfaces, cell_section, axis=0)[:, None]
    amplitude = jnp.take(mode_loss, cell_profile, axis=0)[:, None, :]
    angle = jnp.take(phase, cell_profile, axis=0)
    cells = build_cells(selected, amplitude * jnp.cos(angle), amplitude * jnp.sin(angle))

    unit = jnp.stack(
        [jnp.eye(mode_count, dtype=jnp.float32), jnp.zeros((mode_count, mode_count), jnp.float32)]
    )
    unit = jnp.broadcast_to(unit, (waves_here, 2, mode_count, mode_count))
    zero = jnp.zeros_like(unit)

    local_suffix = suffix_scan(cells)
    local_prefix = prefix_scan(cells[1])
    local_incoming = jnp.concatenate([unit[None], local_prefix[:-1]], axis=0)

    total = jax.tree.map(lambda a: a[0], local_suffix)
    right = (zero, unit, unit)
    left = unit
    shift = 1
    while shift < devices:
        last = shift * 2 >= devices
        perm = [(i, i ^ shift) for i in range(devices)]
        other = lax.ppermute(jnp.stack(total), "cell", perm)
        other = (other[0], other[1], other[2])
        upper = (place & shift) == 0
        first = pick(upper, total, other)
        second = pick(upper, other, total)
        joined = star(
            jax.tree.map(lambda a, b: jnp.stack([a, b]), right, first),
            jax.tree.map(lambda a, b: jnp.stack([a, b]), other, second),
            need_back=not last,
        )
        right = tuple(
            None if n is None else jnp.where(upper, n[0], r) for n, r in zip(joined, right)
        )
        total = tuple(None if n is None else n[1] for n in joined)
        left = jnp.where(upper, left, cmul(left, other[1]))
        shift *= 2

    suffix_refl = local_suffix[0] + cmul(cmul(local_suffix[2], right[0][None]), local_suffix[1])
    suffix_trans = cmul(right[1][None], local_suffix[1])
    incoming = cmul(local_incoming, left[None])

    mismatch = total[1] - target
    fields = incoming + cmul(suffix_refl, incoming)
    adjoint = cmul(jnp.swapaxes(suffix_trans, -1, -2), mismatch[None])
    coupling = jnp.einsum(
        "cwij,cwkj->cik", fields[:, :, 0], adjoint[:, :, 0], precision=HIGHEST
    ) - jnp.einsum("cwij,cwkj->cik", fields[:, :, 1], adjoint[:, :, 1], precision=HIGHEST)
    summed = wl_sum(coupling)
    chosen = jnp.take(mode_field, cell_profile, axis=0)
    weighted = jnp.einsum("cmn,cnx->cmx", summed, chosen, precision=HIGHEST)
    gradient = jnp.sum(chosen * weighted, axis=1)

    row_count = mode_count // devices
    mine = lax.dynamic_slice_in_dim(total[0], place * row_count, row_count, 2)
    return (mine, gradient)


def solution(mesh):
    in_specs = (
        P(),
        P("cell"),
        P("cell"),
        P(),
        P(None, "wl", None),
        P(None, None, "wl"),
        P("wl", None, None, None),
    )
    out_specs = (P("wl", None, "cell", None), P("cell", "wl"))
    return jax.shard_map(body, mesh=mesh, in_specs=in_specs, out_specs=out_specs, check_vma=False)
```

```python
import functools

import jax
import jax.numpy as jnp
from jax import lax
from jax.experimental import pallas as pl
from jax.experimental.pallas import tpu as pltpu
from jax.sharding import PartitionSpec as P

HIGHEST = lax.Precision.HIGHEST


def cmul(left, right):
    parts = jnp.einsum("...pmk,...qkn->...pqmn", left, right, precision=HIGHEST)
    real = parts[..., 0, 0, :, :] - parts[..., 1, 1, :, :]
    imag = parts[..., 0, 1, :, :] + parts[..., 1, 0, :, :]
    return jnp.stack([real, imag], axis=-3)


def star(former, latter, need_back=True):
    refl_f, trans_f, back_f = former
    refl_l, trans_l, back_l = latter
    reflect = refl_f + cmul(cmul(back_f, refl_l), trans_f)
    trans = cmul(trans_l, trans_f)
    back = cmul(back_f, back_l) if need_back else None
    return (reflect, trans, back)


def pick(flag, a, b):
    return jax.tree.map(lambda u, v: jnp.where(flag, u, v), a, b)


def cat(a, b):
    return jax.tree.map(lambda u, v: jnp.concatenate([u, v], axis=0), a, b)


def interleave(even, odd):
    return jnp.stack([even, odd], axis=1).reshape((-1,) + even.shape[1:])


def suffix_scan(cells):
    count = cells[0].shape[0]
    shift = 1
    while shift < count:
        head = jax.tree.map(lambda a: a[: count - shift], cells)
        tail = jax.tree.map(lambda a: a[shift:], cells)
        joined = star(head, tail)
        cells = cat(joined, jax.tree.map(lambda a: a[count - shift :], cells))
        shift *= 2
    return cells


def prefix_scan(trans):
    count = trans.shape[0]
    shift = 1
    while shift < count:
        joined = cmul(trans[shift:], trans[: count - shift])
        trans = jnp.concatenate([trans[:shift], joined], axis=0)
        shift *= 2
    return trans


def build_cells(selected, prop_real, prop_imag):
    forward = selected[:, :, 1]
    backward = selected[:, :, 2]
    row_real = prop_real[..., :, None]
    row_imag = prop_imag[..., :, None]
    trans = jnp.stack(
        [
            row_real * forward[:, :, 0] - row_imag * forward[:, :, 1],
            row_real * forward[:, :, 1] + row_imag * forward[:, :, 0],
        ],
        axis=2,
    )
    col_real = prop_real[..., None, :]
    col_imag = prop_imag[..., None, :]
    back = jnp.stack(
        [
            backward[:, :, 0] * col_real - backward[:, :, 1] * col_imag,
            backward[:, :, 0] * col_imag + backward[:, :, 1] * col_real,
        ],
        axis=2,
    )
    reflect = jnp.broadcast_to(selected[:, :, 0], trans.shape)
    return (reflect, trans, back)


def wl_sum_kernel(count, part_ref, out_ref, held, send_a, recv_a, send_b, recv_b):
    me = lax.axis_index("wl")
    row = lax.axis_index("cell")
    mesh_id = pl.DeviceIdType.MESH

    def link(src, dst, send, recv, peer):
        return pltpu.make_async_remote_copy(
            src_ref=src, dst_ref=dst, send_sem=send, recv_sem=recv,
            device_id=(peer, row), device_id_type=mesh_id,
        )

    barrier = pltpu.get_barrier_semaphore()
    for step in range(1, count):
        peer = lax.rem(me + step, count)
        pl.semaphore_signal(barrier, inc=1, device_id=(peer, row), device_id_type=mesh_id)
    pl.semaphore_wait(barrier, count - 1)

    outgoing = []
    for step in range(1, count):
        peer = lax.rem(me + step, count)
        copy = link(part_ref.at[peer], held.at[me], send_a.at[peer], recv_a.at[me], peer)
        copy.start()
        outgoing.append(copy)
    total = part_ref[me]
    for step in range(1, count):
        source = lax.rem(me + count - step, count)
        link(part_ref.at[source], held.at[source], send_a.at[source], recv_a.at[source], source).wait_recv()
        total = total + held[source]
    out_ref[me] = total
    for copy in outgoing:
        copy.wait_send()

    outgoing = []
    for step in range(1, count):
        peer = lax.rem(me + step, count)
        copy = link(out_ref.at[me], out_ref.at[me], send_b.at[peer], recv_b.at[me], peer)
        copy.start()
        outgoing.append(copy)
    for step in range(1, count):
        source = lax.rem(me + count - step, count)
        link(out_ref.at[source], out_ref.at[source], send_b.at[source], recv_b.at[source], source).wait_recv()
    for copy in outgoing:
        copy.wait_send()


def wl_sum(value):
    count = lax.axis_size("wl")
    lanes = value.shape[-1]
    parts = value.reshape(count, -1, lanes)
    summed = pl.pallas_call(
        functools.partial(wl_sum_kernel, count),
        out_shape=jax.ShapeDtypeStruct(parts.shape, parts.dtype),
        in_specs=[pl.BlockSpec(memory_space=pltpu.VMEM)],
        out_specs=pl.BlockSpec(memory_space=pltpu.VMEM),
        scratch_shapes=[
            pltpu.VMEM(parts.shape, parts.dtype),
            pltpu.SemaphoreType.DMA((count,)),
            pltpu.SemaphoreType.DMA((count,)),
            pltpu.SemaphoreType.DMA((count,)),
            pltpu.SemaphoreType.DMA((count,)),
        ],
        compiler_params=pltpu.CompilerParams(collective_id=0, has_side_effects=True),
    )(parts)
    return summed.reshape(value.shape)


def body(interfaces, cell_profile, cell_section, mode_loss, phase, mode_field, target):
    mode_count = mode_loss.shape[1]
    waves_here = phase.shape[1]
    devices = lax.axis_size("cell")
    place = lax.axis_index("cell")

    selected = jnp.take(interfaces, cell_section, axis=0)[:, None]
    amplitude = jnp.take(mode_loss, cell_profile, axis=0)[:, None, :]
    angle = jnp.take(phase, cell_profile, axis=0)
    cells = build_cells(selected, amplitude * jnp.cos(angle), amplitude * jnp.sin(angle))

    unit = jnp.stack(
        [jnp.eye(mode_count, dtype=jnp.float32), jnp.zeros((mode_count, mode_count), jnp.float32)]
    )
    unit = jnp.broadcast_to(unit, (waves_here, 2, mode_count, mode_count))
    zero = jnp.zeros_like(unit)

    levels = [cells]
    while levels[-1][0].shape[0] > 1:
        nodes = levels[-1]
        levels.append(star(jax.tree.map(lambda a: a[0::2], nodes), jax.tree.map(lambda a: a[1::2], nodes)))
    block = jax.tree.map(lambda a: a[0], levels[-1])

    row_count = mode_count // devices
    total = block
    right = (zero, unit, unit)
    left = unit
    shift = 1
    while shift < devices // 2:
        perm = [(i, i ^ shift) for i in range(devices)]
        other = lax.ppermute(jnp.stack(total), "cell", perm)
        other = (other[0], other[1], other[2])
        upper = (place & shift) == 0
        first = pick(upper, total, other)
        second = pick(upper, other, total)
        joined = star(
            jax.tree.map(lambda a, b: jnp.stack([a, b]), right, first),
            jax.tree.map(lambda a, b: jnp.stack([a, b]), other, second),
        )
        right = pick(upper, jax.tree.map(lambda a: a[0], joined), right)
        total = jax.tree.map(lambda a: a[1], joined)
        left = jnp.where(upper, left, cmul(left, other[1]))
        shift *= 2

    perm = [(i, i ^ shift) for i in range(devices)]
    partner = place ^ shift
    rows_out = lax.dynamic_slice_in_dim(total[2], partner * row_count, row_count, 2)
    sent = jnp.concatenate([total[0], total[1], rows_out], axis=2)
    got = lax.ppermute(sent, "cell", perm)
    other_refl = got[:, :, :mode_count]
    other_trans = got[:, :, mode_count : 2 * mode_count]
    other_rows = got[:, :, 2 * mode_count :]
    upper = (place & shift) == 0
    own_rows = lax.dynamic_slice_in_dim(total[2], place * row_count, row_count, 2)
    first_refl = jnp.where(upper, total[0], other_refl)
    first_trans = jnp.where(upper, total[1], other_trans)
    first_rows = jnp.where(upper, own_rows, other_rows)
    second_refl = jnp.where(upper, other_refl, total[0])
    second_trans = jnp.where(upper, other_trans, total[1])
    joined = star(
        (right[0], right[1], right[2]),
        (other_refl, other_trans, None),
        need_back=False,
    )
    right = (jnp.where(upper, joined[0], right[0]), jnp.where(upper, joined[1], right[1]))
    left = jnp.where(upper, left, cmul(left, other_trans))
    total_trans = cmul(second_trans, first_trans)
    mine = lax.dynamic_slice_in_dim(first_refl, place * row_count, row_count, 2) + cmul(
        cmul(first_rows, second_refl), first_trans
    )

    suffix = levels[-1]
    incoming = unit[None]
    for depth in reversed(range(len(levels) - 1)):
        nodes = levels[depth]
        odd = jax.tree.map(lambda a: a[1::2], nodes)
        if suffix[0].shape[0] > 1:
            joined = star(jax.tree.map(lambda a: a[:-1], odd), jax.tree.map(lambda a: a[1:], suffix))
            odd_suffix = cat(joined, jax.tree.map(lambda a: a[-1:], odd))
        else:
            odd_suffix = odd
        suffix = jax.tree.map(interleave, suffix, odd_suffix)
        incoming = interleave(incoming, cmul(nodes[1][0::2], incoming))
    local_suffix = suffix
    local_incoming = incoming

    suffix_refl = local_suffix[0] + cmul(cmul(local_suffix[2], right[0][None]), local_suffix[1])
    suffix_trans = cmul(right[1][None], local_suffix[1])
    incoming = cmul(local_incoming, left[None])

    mismatch = total_trans - target
    fields = incoming + cmul(suffix_refl, incoming)
    adjoint = cmul(jnp.swapaxes(suffix_trans, -1, -2), mismatch[None])
    coupling = jnp.einsum(
        "cwij,cwkj->cik", fields[:, :, 0], adjoint[:, :, 0], precision=HIGHEST
    ) - jnp.einsum("cwij,cwkj->cik", fields[:, :, 1], adjoint[:, :, 1], precision=HIGHEST)
    summed = wl_sum(coupling)
    chosen = jnp.take(mode_field, cell_profile, axis=0)
    weighted = jnp.einsum("cmn,cnx->cmx", summed, chosen, precision=HIGHEST)
    gradient = jnp.sum(chosen * weighted, axis=1)

    return (mine, gradient)


def solution(mesh):
    in_specs = (
        P(),
        P("cell"),
        P("cell"),
        P(),
        P(None, "wl", None),
        P(None, None, "wl"),
        P("wl", None, None, None),
    )
    out_specs = (P("wl", None, "cell", None), P("cell", "wl"))
    return jax.shard_map(body, mesh=mesh, in_specs=in_specs, out_specs=out_specs, check_vma=False)
```

```python
import functools

import jax
import jax.numpy as jnp
from jax import lax
from jax.experimental import pallas as pl
from jax.experimental.pallas import tpu as pltpu
from jax.sharding import PartitionSpec as P

HIGHEST = lax.Precision.HIGHEST


def cmul(left, right):
    parts = jnp.einsum("...pmk,...qkn->...pqmn", left, right, precision=HIGHEST)
    real = parts[..., 0, 0, :, :] - parts[..., 1, 1, :, :]
    imag = parts[..., 0, 1, :, :] + parts[..., 1, 0, :, :]
    return jnp.stack([real, imag], axis=-3)


def star(former, latter, need_back=True):
    refl_f, trans_f, back_f = former
    refl_l, trans_l, back_l = latter
    reflect = refl_f + cmul(cmul(back_f, refl_l), trans_f)
    trans = cmul(trans_l, trans_f)
    back = cmul(back_f, back_l) if need_back else None
    return (reflect, trans, back)


def pick(flag, a, b):
    return jax.tree.map(lambda u, v: jnp.where(flag, u, v), a, b)


def cat(a, b):
    return jax.tree.map(lambda u, v: jnp.concatenate([u, v], axis=0), a, b)


def interleave(even, odd):
    return jnp.stack([even, odd], axis=1).reshape((-1,) + even.shape[1:])


def suffix_scan(cells):
    count = cells[0].shape[0]
    shift = 1
    while shift < count:
        head = jax.tree.map(lambda a: a[: count - shift], cells)
        tail = jax.tree.map(lambda a: a[shift:], cells)
        joined = star(head, tail)
        cells = cat(joined, jax.tree.map(lambda a: a[count - shift :], cells))
        shift *= 2
    return cells


def prefix_scan(trans):
    count = trans.shape[0]
    shift = 1
    while shift < count:
        joined = cmul(trans[shift:], trans[: count - shift])
        trans = jnp.concatenate([trans[:shift], joined], axis=0)
        shift *= 2
    return trans


def build_cells(selected, prop_real, prop_imag):
    forward = selected[:, :, 1]
    backward = selected[:, :, 2]
    row_real = prop_real[..., :, None]
    row_imag = prop_imag[..., :, None]
    trans = jnp.stack(
        [
            row_real * forward[:, :, 0] - row_imag * forward[:, :, 1],
            row_real * forward[:, :, 1] + row_imag * forward[:, :, 0],
        ],
        axis=2,
    )
    col_real = prop_real[..., None, :]
    col_imag = prop_imag[..., None, :]
    back = jnp.stack(
        [
            backward[:, :, 0] * col_real - backward[:, :, 1] * col_imag,
            backward[:, :, 0] * col_imag + backward[:, :, 1] * col_real,
        ],
        axis=2,
    )
    reflect = jnp.broadcast_to(selected[:, :, 0], trans.shape)
    return (reflect, trans, back)


def wl_sum_kernel(count, part_ref, out_ref, held, send_a, recv_a, send_b, recv_b):
    me = lax.axis_index("wl")
    row = lax.axis_index("cell")
    mesh_id = pl.DeviceIdType.MESH

    def link(src, dst, send, recv, peer):
        return pltpu.make_async_remote_copy(
            src_ref=src, dst_ref=dst, send_sem=send, recv_sem=recv,
            device_id=(peer, row), device_id_type=mesh_id,
        )

    barrier = pltpu.get_barrier_semaphore()
    for step in range(1, count):
        peer = lax.rem(me + step, count)
        pl.semaphore_signal(barrier, inc=1, device_id=(peer, row), device_id_type=mesh_id)
    pl.semaphore_wait(barrier, count - 1)

    outgoing = []
    for step in range(1, count):
        peer = lax.rem(me + step, count)
        copy = link(part_ref.at[peer], held.at[me], send_a.at[peer], recv_a.at[me], peer)
        copy.start()
        outgoing.append(copy)
    total = part_ref[me]
    for step in range(1, count):
        source = lax.rem(me + count - step, count)
        link(part_ref.at[source], held.at[source], send_a.at[source], recv_a.at[source], source).wait_recv()
        total = total + held[source]
    out_ref[me] = total
    for copy in outgoing:
        copy.wait_send()

    outgoing = []
    for step in range(1, count):
        peer = lax.rem(me + step, count)
        copy = link(out_ref.at[me], out_ref.at[me], send_b.at[peer], recv_b.at[me], peer)
        copy.start()
        outgoing.append(copy)
    for step in range(1, count):
        source = lax.rem(me + count - step, count)
        link(out_ref.at[source], out_ref.at[source], send_b.at[source], recv_b.at[source], source).wait_recv()
    for copy in outgoing:
        copy.wait_send()


def wl_sum(value):
    count = lax.axis_size("wl")
    lanes = value.shape[-1]
    parts = value.reshape(count, -1, lanes)
    summed = pl.pallas_call(
        functools.partial(wl_sum_kernel, count),
        out_shape=jax.ShapeDtypeStruct(parts.shape, parts.dtype),
        in_specs=[pl.BlockSpec(memory_space=pltpu.VMEM)],
        out_specs=pl.BlockSpec(memory_space=pltpu.VMEM),
        scratch_shapes=[
            pltpu.VMEM(parts.shape, parts.dtype),
            pltpu.SemaphoreType.DMA((count,)),
            pltpu.SemaphoreType.DMA((count,)),
            pltpu.SemaphoreType.DMA((count,)),
            pltpu.SemaphoreType.DMA((count,)),
        ],
        compiler_params=pltpu.CompilerParams(collective_id=0, has_side_effects=True),
    )(parts)
    return summed.reshape(value.shape)


def body(interfaces, cell_profile, cell_section, mode_loss, phase, mode_field, target):
    mode_count = mode_loss.shape[1]
    waves_here = phase.shape[1]
    devices = lax.axis_size("cell")
    place = lax.axis_index("cell")

    selected = jnp.take(interfaces, cell_section, axis=0)[:, None]
    amplitude = jnp.take(mode_loss, cell_profile, axis=0)[:, None, :]
    angle = jnp.take(phase, cell_profile, axis=0)
    cells = build_cells(selected, amplitude * jnp.cos(angle), amplitude * jnp.sin(angle))

    unit = jnp.stack(
        [jnp.eye(mode_count, dtype=jnp.float32), jnp.zeros((mode_count, mode_count), jnp.float32)]
    )
    unit = jnp.broadcast_to(unit, (waves_here, 2, mode_count, mode_count))
    zero = jnp.zeros_like(unit)

    levels = [cells]
    while levels[-1][0].shape[0] > 1:
        nodes = levels[-1]
        levels.append(star(jax.tree.map(lambda a: a[0::2], nodes), jax.tree.map(lambda a: a[1::2], nodes)))
    block = jax.tree.map(lambda a: a[0], levels[-1])

    def sweep(depth, state):
        suffix, incoming = state
        nodes = levels[depth]
        odd = jax.tree.map(lambda a: a[1::2], nodes)
        if suffix[0].shape[0] > 1:
            joined = star(jax.tree.map(lambda a: a[:-1], odd), jax.tree.map(lambda a: a[1:], suffix))
            odd_suffix = cat(joined, jax.tree.map(lambda a: a[-1:], odd))
        else:
            odd_suffix = odd
        suffix = jax.tree.map(interleave, suffix, odd_suffix)
        incoming = interleave(incoming, cmul(nodes[1][0::2], incoming))
        return (suffix, incoming)

    pending = list(reversed(range(len(levels) - 1)))
    state = (levels[-1], unit[None])

    def overlap(payload, state):
        if not pending:
            return payload, state
        payload, state = lax.optimization_barrier((payload, state))
        return payload, sweep(pending.pop(0), state)

    row_count = mode_count // devices
    total = block
    right = (zero, unit, unit)
    left = unit
    shift = 1
    while shift < devices // 2:
        perm = [(i, i ^ shift) for i in range(devices)]
        payload, state = overlap(jnp.stack(total), state)
        other = lax.ppermute(payload, "cell", perm)
        other = (other[0], other[1], other[2])
        upper = (place & shift) == 0
        first = pick(upper, total, other)
        second = pick(upper, other, total)
        joined = star(
            jax.tree.map(lambda a, b: jnp.stack([a, b]), right, first),
            jax.tree.map(lambda a, b: jnp.stack([a, b]), other, second),
        )
        right = pick(upper, jax.tree.map(lambda a: a[0], joined), right)
        total = jax.tree.map(lambda a: a[1], joined)
        left = jnp.where(upper, left, cmul(left, other[1]))
        shift *= 2

    perm = [(i, i ^ shift) for i in range(devices)]
    partner = place ^ shift
    rows_out = lax.dynamic_slice_in_dim(total[2], partner * row_count, row_count, 2)
    sent = jnp.concatenate([total[0], total[1], rows_out], axis=2)
    sent, state = overlap(sent, state)
    got = lax.ppermute(sent, "cell", perm)
    other_refl = got[:, :, :mode_count]
    other_trans = got[:, :, mode_count : 2 * mode_count]
    other_rows = got[:, :, 2 * mode_count :]
    upper = (place & shift) == 0
    own_rows = lax.dynamic_slice_in_dim(total[2], place * row_count, row_count, 2)
    first_refl = jnp.where(upper, total[0], other_refl)
    first_trans = jnp.where(upper, total[1], other_trans)
    first_rows = jnp.where(upper, own_rows, other_rows)
    second_refl = jnp.where(upper, other_refl, total[0])
    second_trans = jnp.where(upper, other_trans, total[1])
    joined = star(
        (right[0], right[1], right[2]),
        (other_refl, other_trans, None),
        need_back=False,
    )
    right = (jnp.where(upper, joined[0], right[0]), jnp.where(upper, joined[1], right[1]))
    left = jnp.where(upper, left, cmul(left, other_trans))
    total_trans = cmul(second_trans, first_trans)
    mine = lax.dynamic_slice_in_dim(first_refl, place * row_count, row_count, 2) + cmul(
        cmul(first_rows, second_refl), first_trans
    )

    while pending:
        state = sweep(pending.pop(0), state)
    local_suffix, local_incoming = state

    suffix_refl = local_suffix[0] + cmul(cmul(local_suffix[2], right[0][None]), local_suffix[1])
    suffix_trans = cmul(right[1][None], local_suffix[1])
    incoming = cmul(local_incoming, left[None])

    mismatch = total_trans - target
    fields = incoming + cmul(suffix_refl, incoming)
    adjoint = cmul(jnp.swapaxes(suffix_trans, -1, -2), mismatch[None])
    coupling = jnp.einsum(
        "cwij,cwkj->cik", fields[:, :, 0], adjoint[:, :, 0], precision=HIGHEST
    ) - jnp.einsum("cwij,cwkj->cik", fields[:, :, 1], adjoint[:, :, 1], precision=HIGHEST)
    summed = wl_sum(coupling)
    chosen = jnp.take(mode_field, cell_profile, axis=0)
    weighted = jnp.einsum("cmn,cnx->cmx", summed, chosen, precision=HIGHEST)
    gradient = jnp.sum(chosen * weighted, axis=1)

    return (mine, gradient)


def solution(mesh):
    in_specs = (
        P(),
        P("cell"),
        P("cell"),
        P(),
        P(None, "wl", None),
        P(None, None, "wl"),
        P("wl", None, None, None),
    )
    out_specs = (P("wl", None, "cell", None), P("cell", "wl"))
    return jax.shard_map(body, mesh=mesh, in_specs=in_specs, out_specs=out_specs, check_vma=False)
```

```python
import functools

import jax
import jax.numpy as jnp
from jax import lax
from jax.experimental import pallas as pl
from jax.experimental.pallas import tpu as pltpu
from jax.sharding import PartitionSpec as P

HIGHEST = lax.Precision.HIGHEST


def cmul(left, right):
    parts = jnp.einsum("...pmk,...qkn->...pqmn", left, right, precision=HIGHEST)
    real = parts[..., 0, 0, :, :] - parts[..., 1, 1, :, :]
    imag = parts[..., 0, 1, :, :] + parts[..., 1, 0, :, :]
    return jnp.stack([real, imag], axis=-3)


def star(former, latter, need_back=True):
    refl_f, trans_f, back_f = former
    refl_l, trans_l, back_l = latter
    reflect = refl_f + cmul(cmul(back_f, refl_l), trans_f)
    trans = cmul(trans_l, trans_f)
    back = cmul(back_f, back_l) if need_back else None
    return (reflect, trans, back)


def pick(flag, a, b):
    return jax.tree.map(lambda u, v: jnp.where(flag, u, v), a, b)


def cat(a, b):
    return jax.tree.map(lambda u, v: jnp.concatenate([u, v], axis=0), a, b)


def interleave(even, odd):
    return jnp.stack([even, odd], axis=1).reshape((-1,) + even.shape[1:])


def suffix_scan(cells):
    count = cells[0].shape[0]
    shift = 1
    while shift < count:
        head = jax.tree.map(lambda a: a[: count - shift], cells)
        tail = jax.tree.map(lambda a: a[shift:], cells)
        joined = star(head, tail)
        cells = cat(joined, jax.tree.map(lambda a: a[count - shift :], cells))
        shift *= 2
    return cells


def prefix_scan(trans):
    count = trans.shape[0]
    shift = 1
    while shift < count:
        joined = cmul(trans[shift:], trans[: count - shift])
        trans = jnp.concatenate([trans[:shift], joined], axis=0)
        shift *= 2
    return trans


def build_cells(selected, prop_real, prop_imag):
    forward = selected[:, :, 1]
    backward = selected[:, :, 2]
    row_real = prop_real[..., :, None]
    row_imag = prop_imag[..., :, None]
    trans = jnp.stack(
        [
            row_real * forward[:, :, 0] - row_imag * forward[:, :, 1],
            row_real * forward[:, :, 1] + row_imag * forward[:, :, 0],
        ],
        axis=2,
    )
    col_real = prop_real[..., None, :]
    col_imag = prop_imag[..., None, :]
    back = jnp.stack(
        [
            backward[:, :, 0] * col_real - backward[:, :, 1] * col_imag,
            backward[:, :, 0] * col_imag + backward[:, :, 1] * col_real,
        ],
        axis=2,
    )
    reflect = jnp.broadcast_to(selected[:, :, 0], trans.shape)
    return (reflect, trans, back)


def wl_sum_kernel(count, part_ref, out_ref, held, send_a, recv_a, send_b, recv_b):
    me = lax.axis_index("wl")
    row = lax.axis_index("cell")
    mesh_id = pl.DeviceIdType.MESH

    def link(src, dst, send, recv, peer):
        return pltpu.make_async_remote_copy(
            src_ref=src, dst_ref=dst, send_sem=send, recv_sem=recv,
            device_id=(peer, row), device_id_type=mesh_id,
        )

    barrier = pltpu.get_barrier_semaphore()
    for step in range(1, count):
        peer = lax.rem(me + step, count)
        pl.semaphore_signal(barrier, inc=1, device_id=(peer, row), device_id_type=mesh_id)
    pl.semaphore_wait(barrier, count - 1)

    outgoing = []
    for step in range(1, count):
        peer = lax.rem(me + step, count)
        copy = link(part_ref.at[peer], held.at[me], send_a.at[peer], recv_a.at[me], peer)
        copy.start()
        outgoing.append(copy)
    total = part_ref[me]
    for step in range(1, count):
        source = lax.rem(me + count - step, count)
        link(part_ref.at[source], held.at[source], send_a.at[source], recv_a.at[source], source).wait_recv()
        total = total + held[source]
    out_ref[me] = total
    for copy in outgoing:
        copy.wait_send()

    outgoing = []
    for step in range(1, count):
        peer = lax.rem(me + step, count)
        copy = link(out_ref.at[me], out_ref.at[me], send_b.at[peer], recv_b.at[me], peer)
        copy.start()
        outgoing.append(copy)
    for step in range(1, count):
        source = lax.rem(me + count - step, count)
        link(out_ref.at[source], out_ref.at[source], send_b.at[source], recv_b.at[source], source).wait_recv()
    for copy in outgoing:
        copy.wait_send()


def wl_sum(value):
    count = lax.axis_size("wl")
    lanes = value.shape[-1]
    parts = value.reshape(count, -1, lanes)
    summed = pl.pallas_call(
        functools.partial(wl_sum_kernel, count),
        out_shape=jax.ShapeDtypeStruct(parts.shape, parts.dtype),
        in_specs=[pl.BlockSpec(memory_space=pltpu.VMEM)],
        out_specs=pl.BlockSpec(memory_space=pltpu.VMEM),
        scratch_shapes=[
            pltpu.VMEM(parts.shape, parts.dtype),
            pltpu.SemaphoreType.DMA((count,)),
            pltpu.SemaphoreType.DMA((count,)),
            pltpu.SemaphoreType.DMA((count,)),
            pltpu.SemaphoreType.DMA((count,)),
        ],
        compiler_params=pltpu.CompilerParams(collective_id=0, has_side_effects=True),
    )(parts)
    return summed.reshape(value.shape)


def exchange(payload, shift, devices, place):
    perm = [(i, i ^ shift) for i in range(devices)]
    if shift == 1:
        return lax.ppermute(payload, "cell", perm)
    core = place & 1
    half = payload.shape[-2] // 2
    mine = lax.dynamic_slice_in_dim(payload, core * half, half, payload.ndim - 2)
    got = lax.ppermute(mine, "cell", perm)
    sibling = lax.ppermute(got, "cell", [(i, i ^ 1) for i in range(devices)])
    low = jnp.where(core == 0, got, sibling)
    high = jnp.where(core == 0, sibling, got)
    return jnp.concatenate([low, high], axis=payload.ndim - 2)


def body(interfaces, cell_profile, cell_section, mode_loss, phase, mode_field, target):
    mode_count = mode_loss.shape[1]
    waves_here = phase.shape[1]
    devices = lax.axis_size("cell")
    place = lax.axis_index("cell")

    selected = jnp.take(interfaces, cell_section, axis=0)[:, None]
    amplitude = jnp.take(mode_loss, cell_profile, axis=0)[:, None, :]
    angle = jnp.take(phase, cell_profile, axis=0)
    cells = build_cells(selected, amplitude * jnp.cos(angle), amplitude * jnp.sin(angle))

    unit = jnp.stack(
        [jnp.eye(mode_count, dtype=jnp.float32), jnp.zeros((mode_count, mode_count), jnp.float32)]
    )
    unit = jnp.broadcast_to(unit, (waves_here, 2, mode_count, mode_count))
    zero = jnp.zeros_like(unit)

    levels = [cells]
    while levels[-1][0].shape[0] > 1:
        nodes = levels[-1]
        levels.append(star(jax.tree.map(lambda a: a[0::2], nodes), jax.tree.map(lambda a: a[1::2], nodes)))
    block = jax.tree.map(lambda a: a[0], levels[-1])

    def sweep(depth, state):
        suffix, incoming = state
        nodes = levels[depth]
        odd = jax.tree.map(lambda a: a[1::2], nodes)
        if suffix[0].shape[0] > 1:
            joined = star(jax.tree.map(lambda a: a[:-1], odd), jax.tree.map(lambda a: a[1:], suffix))
            odd_suffix = cat(joined, jax.tree.map(lambda a: a[-1:], odd))
        else:
            odd_suffix = odd
        suffix = jax.tree.map(interleave, suffix, odd_suffix)
        incoming = interleave(incoming, cmul(nodes[1][0::2], incoming))
        return (suffix, incoming)

    pending = list(reversed(range(len(levels) - 1)))
    state = (levels[-1], unit[None])

    def overlap(payload, state):
        if not pending:
            return payload, state
        payload, state = lax.optimization_barrier((payload, state))
        return payload, sweep(pending.pop(0), state)

    row_count = mode_count // devices
    total = block
    right = (zero, unit, unit)
    left = unit
    shift = 1
    while shift < devices // 2:
        perm = [(i, i ^ shift) for i in range(devices)]
        payload, state = overlap(jnp.stack(total), state)
        other = exchange(payload, shift, devices, place)
        other = (other[0], other[1], other[2])
        upper = (place & shift) == 0
        first = pick(upper, total, other)
        second = pick(upper, other, total)
        joined = star(
            jax.tree.map(lambda a, b: jnp.stack([a, b]), right, first),
            jax.tree.map(lambda a, b: jnp.stack([a, b]), other, second),
        )
        right = pick(upper, jax.tree.map(lambda a: a[0], joined), right)
        total = jax.tree.map(lambda a: a[1], joined)
        left = jnp.where(upper, left, cmul(left, other[1]))
        shift *= 2

    perm = [(i, i ^ shift) for i in range(devices)]
    partner = place ^ shift
    pair = 2 if shift > 1 else 1
    rows_out = lax.dynamic_slice_in_dim(total[2], (partner - (partner % pair)) * row_count, pair * row_count, 2)
    sent = jnp.concatenate([total[0], total[1], rows_out], axis=2)
    sent, state = overlap(sent, state)
    got = exchange(sent, shift, devices, place)
    other_refl = got[:, :, :mode_count]
    other_trans = got[:, :, mode_count : 2 * mode_count]
    other_rows = lax.dynamic_slice_in_dim(got, 2 * mode_count + (place % pair) * row_count, row_count, 2)
    upper = (place & shift) == 0
    own_rows = lax.dynamic_slice_in_dim(total[2], place * row_count, row_count, 2)
    first_refl = jnp.where(upper, total[0], other_refl)
    first_trans = jnp.where(upper, total[1], other_trans)
    first_rows = jnp.where(upper, own_rows, other_rows)
    second_refl = jnp.where(upper, other_refl, total[0])
    second_trans = jnp.where(upper, other_trans, total[1])
    joined = star(
        (right[0], right[1], right[2]),
        (other_refl, other_trans, None),
        need_back=False,
    )
    right = (jnp.where(upper, joined[0], right[0]), jnp.where(upper, joined[1], right[1]))
    left = jnp.where(upper, left, cmul(left, other_trans))
    total_trans = cmul(second_trans, first_trans)
    mine = lax.dynamic_slice_in_dim(first_refl, place * row_count, row_count, 2) + cmul(
        cmul(first_rows, second_refl), first_trans
    )

    while pending:
        state = sweep(pending.pop(0), state)
    local_suffix, local_incoming = state

    suffix_refl = local_suffix[0] + cmul(cmul(local_suffix[2], right[0][None]), local_suffix[1])
    suffix_trans = cmul(right[1][None], local_suffix[1])
    incoming = cmul(local_incoming, left[None])

    mismatch = total_trans - target
    fields = incoming + cmul(suffix_refl, incoming)
    adjoint = cmul(jnp.swapaxes(suffix_trans, -1, -2), mismatch[None])
    coupling = jnp.einsum(
        "cwij,cwkj->cik", fields[:, :, 0], adjoint[:, :, 0], precision=HIGHEST
    ) - jnp.einsum("cwij,cwkj->cik", fields[:, :, 1], adjoint[:, :, 1], precision=HIGHEST)
    summed = wl_sum(coupling)
    chosen = jnp.take(mode_field, cell_profile, axis=0)
    weighted = jnp.einsum("cmn,cnx->cmx", summed, chosen, precision=HIGHEST)
    gradient = jnp.sum(chosen * weighted, axis=1)

    return (mine, gradient)


def solution(mesh):
    in_specs = (
        P(),
        P("cell"),
        P("cell"),
        P(),
        P(None, "wl", None),
        P(None, None, "wl"),
        P("wl", None, None, None),
    )
    out_specs = (P("wl", None, "cell", None), P("cell", "wl"))
    return jax.shard_map(body, mesh=mesh, in_specs=in_specs, out_specs=out_specs, check_vma=False)
```

```python
import functools

import jax
import jax.numpy as jnp
from jax import lax
from jax.experimental import pallas as pl
from jax.experimental.pallas import tpu as pltpu
from jax.sharding import PartitionSpec as P

HIGHEST = lax.Precision.HIGHEST


def cmul(left, right):
    parts = jnp.einsum("...pmk,...qkn->...pqmn", left, right, precision=HIGHEST)
    real = parts[..., 0, 0, :, :] - parts[..., 1, 1, :, :]
    imag = parts[..., 0, 1, :, :] + parts[..., 1, 0, :, :]
    return jnp.stack([real, imag], axis=-3)


def star(former, latter, need_back=True):
    refl_f, trans_f, back_f = former
    refl_l, trans_l, back_l = latter
    reflect = refl_f + cmul(cmul(back_f, refl_l), trans_f)
    trans = cmul(trans_l, trans_f)
    back = cmul(back_f, back_l) if need_back else None
    return (reflect, trans, back)


def pick(flag, a, b):
    return jax.tree.map(lambda u, v: jnp.where(flag, u, v), a, b)


def cat(a, b):
    return jax.tree.map(lambda u, v: jnp.concatenate([u, v], axis=0), a, b)


def interleave(even, odd):
    return jnp.stack([even, odd], axis=1).reshape((-1,) + even.shape[1:])


def suffix_scan(cells):
    count = cells[0].shape[0]
    shift = 1
    while shift < count:
        head = jax.tree.map(lambda a: a[: count - shift], cells)
        tail = jax.tree.map(lambda a: a[shift:], cells)
        joined = star(head, tail)
        cells = cat(joined, jax.tree.map(lambda a: a[count - shift :], cells))
        shift *= 2
    return cells


def prefix_scan(trans):
    count = trans.shape[0]
    shift = 1
    while shift < count:
        joined = cmul(trans[shift:], trans[: count - shift])
        trans = jnp.concatenate([trans[:shift], joined], axis=0)
        shift *= 2
    return trans


def build_cells(selected, prop_real, prop_imag):
    forward = selected[:, :, 1]
    backward = selected[:, :, 2]
    row_real = prop_real[..., :, None]
    row_imag = prop_imag[..., :, None]
    trans = jnp.stack(
        [
            row_real * forward[:, :, 0] - row_imag * forward[:, :, 1],
            row_real * forward[:, :, 1] + row_imag * forward[:, :, 0],
        ],
        axis=2,
    )
    col_real = prop_real[..., None, :]
    col_imag = prop_imag[..., None, :]
    back = jnp.stack(
        [
            backward[:, :, 0] * col_real - backward[:, :, 1] * col_imag,
            backward[:, :, 0] * col_imag + backward[:, :, 1] * col_real,
        ],
        axis=2,
    )
    reflect = jnp.broadcast_to(selected[:, :, 0], trans.shape)
    return (reflect, trans, back)


def wl_sum_kernel(count, part_ref, out_ref, held, send_a, recv_a, send_b, recv_b):
    me = lax.axis_index("wl")
    row = lax.axis_index("cell")
    mesh_id = pl.DeviceIdType.MESH

    def link(src, dst, send, recv, peer):
        return pltpu.make_async_remote_copy(
            src_ref=src, dst_ref=dst, send_sem=send, recv_sem=recv,
            device_id=(peer, row), device_id_type=mesh_id,
        )

    barrier = pltpu.get_barrier_semaphore()
    for step in range(1, count):
        peer = lax.rem(me + step, count)
        pl.semaphore_signal(barrier, inc=1, device_id=(peer, row), device_id_type=mesh_id)
    pl.semaphore_wait(barrier, count - 1)

    outgoing = []
    for step in range(1, count):
        peer = lax.rem(me + step, count)
        copy = link(part_ref.at[peer], held.at[me], send_a.at[peer], recv_a.at[me], peer)
        copy.start()
        outgoing.append(copy)
    total = part_ref[me]
    for step in range(1, count):
        source = lax.rem(me + count - step, count)
        link(part_ref.at[source], held.at[source], send_a.at[source], recv_a.at[source], source).wait_recv()
        total = total + held[source]
    out_ref[me] = total
    for copy in outgoing:
        copy.wait_send()

    outgoing = []
    for step in range(1, count):
        peer = lax.rem(me + step, count)
        copy = link(out_ref.at[me], out_ref.at[me], send_b.at[peer], recv_b.at[me], peer)
        copy.start()
        outgoing.append(copy)
    for step in range(1, count):
        source = lax.rem(me + count - step, count)
        link(out_ref.at[source], out_ref.at[source], send_b.at[source], recv_b.at[source], source).wait_recv()
    for copy in outgoing:
        copy.wait_send()


def wl_sum(value):
    count = lax.axis_size("wl")
    lanes = value.shape[-1]
    parts = value.reshape(count, -1, lanes)
    summed = pl.pallas_call(
        functools.partial(wl_sum_kernel, count),
        out_shape=jax.ShapeDtypeStruct(parts.shape, parts.dtype),
        in_specs=[pl.BlockSpec(memory_space=pltpu.VMEM)],
        out_specs=pl.BlockSpec(memory_space=pltpu.VMEM),
        scratch_shapes=[
            pltpu.VMEM(parts.shape, parts.dtype),
            pltpu.SemaphoreType.DMA((count,)),
            pltpu.SemaphoreType.DMA((count,)),
            pltpu.SemaphoreType.DMA((count,)),
            pltpu.SemaphoreType.DMA((count,)),
        ],
        compiler_params=pltpu.CompilerParams(collective_id=0, has_side_effects=True),
    )(parts)
    return summed.reshape(value.shape)


def exchange(payload, shift, devices, place):
    perm = [(i, i ^ shift) for i in range(devices)]
    if shift == 1:
        return lax.ppermute(payload, "cell", perm)
    core = place & 1
    half = payload.shape[-2] // 2
    mine = lax.dynamic_slice_in_dim(payload, core * half, half, payload.ndim - 2)
    got = lax.ppermute(mine, "cell", perm)
    sibling = lax.ppermute(got, "cell", [(i, i ^ 1) for i in range(devices)])
    low = jnp.where(core == 0, got, sibling)
    high = jnp.where(core == 0, sibling, got)
    return jnp.concatenate([low, high], axis=payload.ndim - 2)


def body(interfaces, cell_profile, cell_section, mode_loss, phase, mode_field, target):
    mode_count = mode_loss.shape[1]
    waves_here = phase.shape[1]
    devices = lax.axis_size("cell")
    place = lax.axis_index("cell")

    selected = jnp.take(interfaces, cell_section, axis=0)[:, None]
    amplitude = jnp.take(mode_loss, cell_profile, axis=0)[:, None, :]
    angle = jnp.take(phase, cell_profile, axis=0)
    cells = build_cells(selected, amplitude * jnp.cos(angle), amplitude * jnp.sin(angle))

    unit = jnp.stack(
        [jnp.eye(mode_count, dtype=jnp.float32), jnp.zeros((mode_count, mode_count), jnp.float32)]
    )
    unit = jnp.broadcast_to(unit, (waves_here, 2, mode_count, mode_count))
    zero = jnp.zeros_like(unit)

    levels = [cells]
    while levels[-1][0].shape[0] > 1:
        nodes = levels[-1]
        levels.append(star(jax.tree.map(lambda a: a[0::2], nodes), jax.tree.map(lambda a: a[1::2], nodes)))
    block = jax.tree.map(lambda a: a[0], levels[-1])

    def sweep(depth, state):
        suffix, incoming = state
        nodes = levels[depth]
        odd = jax.tree.map(lambda a: a[1::2], nodes)
        if suffix[0].shape[0] > 1:
            joined = star(jax.tree.map(lambda a: a[:-1], odd), jax.tree.map(lambda a: a[1:], suffix))
            odd_suffix = cat(joined, jax.tree.map(lambda a: a[-1:], odd))
        else:
            odd_suffix = odd
        suffix = jax.tree.map(interleave, suffix, odd_suffix)
        incoming = interleave(incoming, cmul(nodes[1][0::2], incoming))
        return (suffix, incoming)

    pending = list(reversed(range(len(levels) - 1)))
    state = (levels[-1], unit[None])

    def overlap(payload, state):
        if not pending:
            return payload, state
        payload, state = lax.optimization_barrier((payload, state))
        return payload, sweep(pending.pop(0), state)

    row_count = mode_count // devices
    total = block
    right = (zero, unit, unit)
    left = unit
    shift = 1
    while shift < devices // 2:
        perm = [(i, i ^ shift) for i in range(devices)]
        payload, state = overlap(jnp.stack(total), state)
        other = exchange(payload, shift, devices, place)
        other = (other[0], other[1], other[2])
        upper = (place & shift) == 0
        first = pick(upper, total, other)
        second = pick(upper, other, total)
        joined = star(
            jax.tree.map(lambda a, b: jnp.stack([a, b]), right, first),
            jax.tree.map(lambda a, b: jnp.stack([a, b]), other, second),
        )
        right = pick(upper, jax.tree.map(lambda a: a[0], joined), right)
        total = jax.tree.map(lambda a: a[1], joined)
        left = jnp.where(upper, left, cmul(left, other[1]))
        shift *= 2

    perm = [(i, i ^ shift) for i in range(devices)]
    partner = place ^ shift
    pair = 2 if shift > 1 else 1
    rows_out = lax.dynamic_slice_in_dim(total[2], (partner - (partner % pair)) * row_count, pair * row_count, 2)
    sent = jnp.concatenate([total[0], total[1], rows_out], axis=2)
    sent, state = overlap(sent, state)
    while pending:
        state = sweep(pending.pop(0), state)
    sent, (local_suffix, local_incoming, right, left) = lax.optimization_barrier(
        (sent, (state[0], state[1], right, left))
    )
    cell_refl, cell_trans, cell_back = local_suffix
    carry_refl, carry_trans, carry_back = right
    refl_before = cell_refl + cmul(cmul(cell_back, carry_refl[None]), cell_trans)
    back_carry = cmul(cell_back, carry_back[None])
    trans_after = cmul(carry_trans[None], cell_trans)
    incoming_before = cmul(local_incoming, left[None])

    got = exchange(sent, shift, devices, place)
    other_refl = got[:, :, :mode_count]
    other_trans = got[:, :, mode_count : 2 * mode_count]
    other_rows = lax.dynamic_slice_in_dim(got, 2 * mode_count + (place % pair) * row_count, row_count, 2)
    upper = (place & shift) == 0
    own_rows = lax.dynamic_slice_in_dim(total[2], place * row_count, row_count, 2)
    first_refl = jnp.where(upper, total[0], other_refl)
    first_trans = jnp.where(upper, total[1], other_trans)
    first_rows = jnp.where(upper, own_rows, other_rows)
    second_refl = jnp.where(upper, other_refl, total[0])
    second_trans = jnp.where(upper, other_trans, total[1])
    total_trans = cmul(second_trans, first_trans)
    mine = lax.dynamic_slice_in_dim(first_refl, place * row_count, row_count, 2) + cmul(
        cmul(first_rows, second_refl), first_trans
    )

    suffix_refl = jnp.where(
        upper, refl_before + cmul(cmul(back_carry, other_refl[None]), trans_after), refl_before
    )
    suffix_trans = jnp.where(upper, cmul(other_trans[None], trans_after), trans_after)
    incoming = jnp.where(upper, incoming_before, cmul(incoming_before, other_trans[None]))

    mismatch = total_trans - target
    fields = incoming + cmul(suffix_refl, incoming)
    adjoint = cmul(jnp.swapaxes(suffix_trans, -1, -2), mismatch[None])
    coupling = jnp.einsum(
        "cwij,cwkj->cik", fields[:, :, 0], adjoint[:, :, 0], precision=HIGHEST
    ) - jnp.einsum("cwij,cwkj->cik", fields[:, :, 1], adjoint[:, :, 1], precision=HIGHEST)
    summed = wl_sum(coupling)
    chosen = jnp.take(mode_field, cell_profile, axis=0)
    weighted = jnp.einsum("cmn,cnx->cmx", summed, chosen, precision=HIGHEST)
    gradient = jnp.sum(chosen * weighted, axis=1)

    return (mine, gradient)


def solution(mesh):
    in_specs = (
        P(),
        P("cell"),
        P("cell"),
        P(),
        P(None, "wl", None),
        P(None, None, "wl"),
        P("wl", None, None, None),
    )
    out_specs = (P("wl", None, "cell", None), P("cell", "wl"))
    return jax.shard_map(body, mesh=mesh, in_specs=in_specs, out_specs=out_specs, check_vma=False)
```

```python
import functools

import jax
import jax.numpy as jnp
from jax import lax
from jax.experimental import pallas as pl
from jax.experimental.pallas import tpu as pltpu
from jax.sharding import PartitionSpec as P

HIGHEST = lax.Precision.HIGHEST


def cmul(left, right):
    parts = jnp.einsum("...pmk,...qkn->...pqmn", left, right, precision=HIGHEST)
    real = parts[..., 0, 0, :, :] - parts[..., 1, 1, :, :]
    imag = parts[..., 0, 1, :, :] + parts[..., 1, 0, :, :]
    return jnp.stack([real, imag], axis=-3)


def star(former, latter, need_back=True):
    refl_f, trans_f, back_f = former
    refl_l, trans_l, back_l = latter
    reflect = refl_f + cmul(cmul(back_f, refl_l), trans_f)
    trans = cmul(trans_l, trans_f)
    back = cmul(back_f, back_l) if need_back else None
    return (reflect, trans, back)


def pick(flag, a, b):
    return jax.tree.map(lambda u, v: jnp.where(flag, u, v), a, b)


def cat(a, b):
    return jax.tree.map(lambda u, v: jnp.concatenate([u, v], axis=0), a, b)


def interleave(even, odd):
    return jnp.stack([even, odd], axis=1).reshape((-1,) + even.shape[1:])


def suffix_scan(cells):
    count = cells[0].shape[0]
    shift = 1
    while shift < count:
        head = jax.tree.map(lambda a: a[: count - shift], cells)
        tail = jax.tree.map(lambda a: a[shift:], cells)
        joined = star(head, tail)
        cells = cat(joined, jax.tree.map(lambda a: a[count - shift :], cells))
        shift *= 2
    return cells


def prefix_scan(trans):
    count = trans.shape[0]
    shift = 1
    while shift < count:
        joined = cmul(trans[shift:], trans[: count - shift])
        trans = jnp.concatenate([trans[:shift], joined], axis=0)
        shift *= 2
    return trans


def build_cells(selected, prop_real, prop_imag):
    forward = selected[:, :, 1]
    backward = selected[:, :, 2]
    row_real = prop_real[..., :, None]
    row_imag = prop_imag[..., :, None]
    trans = jnp.stack(
        [
            row_real * forward[:, :, 0] - row_imag * forward[:, :, 1],
            row_real * forward[:, :, 1] + row_imag * forward[:, :, 0],
        ],
        axis=2,
    )
    col_real = prop_real[..., None, :]
    col_imag = prop_imag[..., None, :]
    back = jnp.stack(
        [
            backward[:, :, 0] * col_real - backward[:, :, 1] * col_imag,
            backward[:, :, 0] * col_imag + backward[:, :, 1] * col_real,
        ],
        axis=2,
    )
    reflect = jnp.broadcast_to(selected[:, :, 0], trans.shape)
    return (reflect, trans, back)


def wl_sum_kernel(count, part_ref, out_ref, held, send_a, recv_a, send_b, recv_b):
    me = lax.axis_index("wl")
    row = lax.axis_index("cell")
    mesh_id = pl.DeviceIdType.MESH

    def link(src, dst, send, recv, peer):
        return pltpu.make_async_remote_copy(
            src_ref=src, dst_ref=dst, send_sem=send, recv_sem=recv,
            device_id=(peer, row), device_id_type=mesh_id,
        )

    barrier = pltpu.get_barrier_semaphore()
    for step in range(1, count):
        peer = lax.rem(me + step, count)
        pl.semaphore_signal(barrier, inc=1, device_id=(peer, row), device_id_type=mesh_id)
    pl.semaphore_wait(barrier, count - 1)

    outgoing = []
    for step in range(1, count):
        peer = lax.rem(me + step, count)
        copy = link(part_ref.at[peer], held.at[me], send_a.at[peer], recv_a.at[me], peer)
        copy.start()
        outgoing.append(copy)
    total = part_ref[me]
    for step in range(1, count):
        source = lax.rem(me + count - step, count)
        link(part_ref.at[source], held.at[source], send_a.at[source], recv_a.at[source], source).wait_recv()
        total = total + held[source]
    out_ref[me] = total
    for copy in outgoing:
        copy.wait_send()

    outgoing = []
    for step in range(1, count):
        peer = lax.rem(me + step, count)
        copy = link(out_ref.at[me], out_ref.at[me], send_b.at[peer], recv_b.at[me], peer)
        copy.start()
        outgoing.append(copy)
    for step in range(1, count):
        source = lax.rem(me + count - step, count)
        link(out_ref.at[source], out_ref.at[source], send_b.at[source], recv_b.at[source], source).wait_recv()
    for copy in outgoing:
        copy.wait_send()


def wl_sum(value):
    count = lax.axis_size("wl")
    lanes = value.shape[-1]
    parts = value.reshape(count, -1, lanes)
    summed = pl.pallas_call(
        functools.partial(wl_sum_kernel, count),
        out_shape=jax.ShapeDtypeStruct(parts.shape, parts.dtype),
        in_specs=[pl.BlockSpec(memory_space=pltpu.VMEM)],
        out_specs=pl.BlockSpec(memory_space=pltpu.VMEM),
        scratch_shapes=[
            pltpu.VMEM(parts.shape, parts.dtype),
            pltpu.SemaphoreType.DMA((count,)),
            pltpu.SemaphoreType.DMA((count,)),
            pltpu.SemaphoreType.DMA((count,)),
            pltpu.SemaphoreType.DMA((count,)),
        ],
        compiler_params=pltpu.CompilerParams(collective_id=0, has_side_effects=True),
    )(parts)
    return summed.reshape(value.shape)


def exchange(payload, shift, devices, place):
    perm = [(i, i ^ shift) for i in range(devices)]
    if shift == 1:
        return lax.ppermute(payload, "cell", perm)
    core = place & 1
    half = payload.shape[-2] // 2
    mine = lax.dynamic_slice_in_dim(payload, core * half, half, payload.ndim - 2)
    got = lax.ppermute(mine, "cell", perm)
    sibling = lax.ppermute(got, "cell", [(i, i ^ 1) for i in range(devices)])
    low = jnp.where(core == 0, got, sibling)
    high = jnp.where(core == 0, sibling, got)
    return jnp.concatenate([low, high], axis=payload.ndim - 2)


def body(interfaces, cell_profile, cell_section, mode_loss, phase, mode_field, target):
    mode_count = mode_loss.shape[1]
    waves_here = phase.shape[1]
    devices = lax.axis_size("cell")
    place = lax.axis_index("cell")

    selected = jnp.take(interfaces, cell_section, axis=0)[:, None]
    amplitude = jnp.take(mode_loss, cell_profile, axis=0)[:, None, :]
    angle = jnp.take(phase, cell_profile, axis=0)
    cells = build_cells(selected, amplitude * jnp.cos(angle), amplitude * jnp.sin(angle))

    unit = jnp.stack(
        [jnp.eye(mode_count, dtype=jnp.float32), jnp.zeros((mode_count, mode_count), jnp.float32)]
    )
    unit = jnp.broadcast_to(unit, (waves_here, 2, mode_count, mode_count))
    zero = jnp.zeros_like(unit)

    local_suffix = suffix_scan(cells)
    local_prefix = prefix_scan(cells[1])
    local_incoming = jnp.concatenate([unit[None], local_prefix[:-1]], axis=0)
    block = jax.tree.map(lambda a: a[0], local_suffix)

    row_count = mode_count // devices
    total = block
    right = (zero, unit, unit)
    left = unit
    shift = 1
    while shift < devices // 2:
        perm = [(i, i ^ shift) for i in range(devices)]
        other = exchange(jnp.stack(total), shift, devices, place)
        other = (other[0], other[1], other[2])
        upper = (place & shift) == 0
        first = pick(upper, total, other)
        second = pick(upper, other, total)
        joined = star(
            jax.tree.map(lambda a, b: jnp.stack([a, b]), right, first),
            jax.tree.map(lambda a, b: jnp.stack([a, b]), other, second),
        )
        right = pick(upper, jax.tree.map(lambda a: a[0], joined), right)
        total = jax.tree.map(lambda a: a[1], joined)
        left = jnp.where(upper, left, cmul(left, other[1]))
        shift *= 2

    perm = [(i, i ^ shift) for i in range(devices)]
    partner = place ^ shift
    pair = 2 if shift > 1 else 1
    rows_out = lax.dynamic_slice_in_dim(total[2], (partner - (partner % pair)) * row_count, pair * row_count, 2)
    sent = jnp.concatenate([total[0], total[1], rows_out], axis=2)
    got = exchange(sent, shift, devices, place)
    other_refl = got[:, :, :mode_count]
    other_trans = got[:, :, mode_count : 2 * mode_count]
    other_rows = lax.dynamic_slice_in_dim(got, 2 * mode_count + (place % pair) * row_count, row_count, 2)
    upper = (place & shift) == 0
    own_rows = lax.dynamic_slice_in_dim(total[2], place * row_count, row_count, 2)
    first_refl = jnp.where(upper, total[0], other_refl)
    first_trans = jnp.where(upper, total[1], other_trans)
    first_rows = jnp.where(upper, own_rows, other_rows)
    second_refl = jnp.where(upper, other_refl, total[0])
    second_trans = jnp.where(upper, other_trans, total[1])
    joined = star(
        (right[0], right[1], right[2]),
        (other_refl, other_trans, None),
        need_back=False,
    )
    right = (jnp.where(upper, joined[0], right[0]), jnp.where(upper, joined[1], right[1]))
    left = jnp.where(upper, left, cmul(left, other_trans))
    total_trans = cmul(second_trans, first_trans)
    mine = lax.dynamic_slice_in_dim(first_refl, place * row_count, row_count, 2) + cmul(
        cmul(first_rows, second_refl), first_trans
    )


    suffix_refl = local_suffix[0] + cmul(cmul(local_suffix[2], right[0][None]), local_suffix[1])
    suffix_trans = cmul(right[1][None], local_suffix[1])
    incoming = cmul(local_incoming, left[None])

    mismatch = total_trans - target
    fields = incoming + cmul(suffix_refl, incoming)
    adjoint = cmul(jnp.swapaxes(suffix_trans, -1, -2), mismatch[None])
    coupling = jnp.einsum(
        "cwij,cwkj->cik", fields[:, :, 0], adjoint[:, :, 0], precision=HIGHEST
    ) - jnp.einsum("cwij,cwkj->cik", fields[:, :, 1], adjoint[:, :, 1], precision=HIGHEST)
    summed = wl_sum(coupling)
    chosen = jnp.take(mode_field, cell_profile, axis=0)
    weighted = jnp.einsum("cmn,cnx->cmx", summed, chosen, precision=HIGHEST)
    gradient = jnp.sum(chosen * weighted, axis=1)

    return (mine, gradient)


def solution(mesh):
    in_specs = (
        P(),
        P("cell"),
        P("cell"),
        P(),
        P(None, "wl", None),
        P(None, None, "wl"),
        P("wl", None, None, None),
    )
    out_specs = (P("wl", None, "cell", None), P("cell", "wl"))
    return jax.shard_map(body, mesh=mesh, in_specs=in_specs, out_specs=out_specs, check_vma=False)
```

```python
import functools

import jax
import jax.numpy as jnp
from jax import lax
from jax.experimental import pallas as pl
from jax.experimental.pallas import tpu as pltpu
from jax.sharding import PartitionSpec as P

HIGHEST = lax.Precision.HIGHEST


def cmul(left, right):
    parts = jnp.einsum("...pmk,...qkn->...pqmn", left, right, precision=HIGHEST)
    real = parts[..., 0, 0, :, :] - parts[..., 1, 1, :, :]
    imag = parts[..., 0, 1, :, :] + parts[..., 1, 0, :, :]
    return jnp.stack([real, imag], axis=-3)


def star(former, latter, need_back=True):
    refl_f, trans_f, back_f = former
    refl_l, trans_l, back_l = latter
    reflect = refl_f + cmul(cmul(back_f, refl_l), trans_f)
    trans = cmul(trans_l, trans_f)
    back = cmul(back_f, back_l) if need_back else None
    return (reflect, trans, back)


def pick(flag, a, b):
    return jax.tree.map(lambda u, v: jnp.where(flag, u, v), a, b)


def cat(a, b):
    return jax.tree.map(lambda u, v: jnp.concatenate([u, v], axis=0), a, b)


def interleave(even, odd):
    return jnp.stack([even, odd], axis=1).reshape((-1,) + even.shape[1:])


def suffix_scan(cells):
    count = cells[0].shape[0]
    shift = 1
    while shift < count:
        head = jax.tree.map(lambda a: a[: count - shift], cells)
        tail = jax.tree.map(lambda a: a[shift:], cells)
        joined = star(head, tail)
        cells = cat(joined, jax.tree.map(lambda a: a[count - shift :], cells))
        shift *= 2
    return cells


def prefix_scan(trans):
    count = trans.shape[0]
    shift = 1
    while shift < count:
        joined = cmul(trans[shift:], trans[: count - shift])
        trans = jnp.concatenate([trans[:shift], joined], axis=0)
        shift *= 2
    return trans


def build_cells(selected, prop_real, prop_imag):
    forward = selected[:, :, 1]
    backward = selected[:, :, 2]
    row_real = prop_real[..., :, None]
    row_imag = prop_imag[..., :, None]
    trans = jnp.stack(
        [
            row_real * forward[:, :, 0] - row_imag * forward[:, :, 1],
            row_real * forward[:, :, 1] + row_imag * forward[:, :, 0],
        ],
        axis=2,
    )
    col_real = prop_real[..., None, :]
    col_imag = prop_imag[..., None, :]
    back = jnp.stack(
        [
            backward[:, :, 0] * col_real - backward[:, :, 1] * col_imag,
            backward[:, :, 0] * col_imag + backward[:, :, 1] * col_real,
        ],
        axis=2,
    )
    reflect = jnp.broadcast_to(selected[:, :, 0], trans.shape)
    return (reflect, trans, back)


def wl_sum_kernel(count, part_ref, out_ref, held, send_a, recv_a, send_b, recv_b):
    me = lax.axis_index("wl")
    row = lax.axis_index("cell")
    mesh_id = pl.DeviceIdType.MESH

    def link(src, dst, send, recv, peer):
        return pltpu.make_async_remote_copy(
            src_ref=src, dst_ref=dst, send_sem=send, recv_sem=recv,
            device_id=(peer, row), device_id_type=mesh_id,
        )

    barrier = pltpu.get_barrier_semaphore()
    for step in range(1, count):
        peer = lax.rem(me + step, count)
        pl.semaphore_signal(barrier, inc=1, device_id=(peer, row), device_id_type=mesh_id)
    pl.semaphore_wait(barrier, count - 1)

    outgoing = []
    for step in range(1, count):
        peer = lax.rem(me + step, count)
        copy = link(part_ref.at[peer], held.at[me], send_a.at[peer], recv_a.at[me], peer)
        copy.start()
        outgoing.append(copy)
    total = part_ref[me]
    for step in range(1, count):
        source = lax.rem(me + count - step, count)
        link(part_ref.at[source], held.at[source], send_a.at[source], recv_a.at[source], source).wait_recv()
        total = total + held[source]
    out_ref[me] = total
    for copy in outgoing:
        copy.wait_send()

    outgoing = []
    for step in range(1, count):
        peer = lax.rem(me + step, count)
        copy = link(out_ref.at[me], out_ref.at[me], send_b.at[peer], recv_b.at[me], peer)
        copy.start()
        outgoing.append(copy)
    for step in range(1, count):
        source = lax.rem(me + count - step, count)
        link(out_ref.at[source], out_ref.at[source], send_b.at[source], recv_b.at[source], source).wait_recv()
    for copy in outgoing:
        copy.wait_send()


def wl_sum(value):
    count = lax.axis_size("wl")
    lanes = value.shape[-1]
    parts = value.reshape(count, -1, lanes)
    summed = pl.pallas_call(
        functools.partial(wl_sum_kernel, count),
        out_shape=jax.ShapeDtypeStruct(parts.shape, parts.dtype),
        in_specs=[pl.BlockSpec(memory_space=pltpu.VMEM)],
        out_specs=pl.BlockSpec(memory_space=pltpu.VMEM),
        scratch_shapes=[
            pltpu.VMEM(parts.shape, parts.dtype),
            pltpu.SemaphoreType.DMA((count,)),
            pltpu.SemaphoreType.DMA((count,)),
            pltpu.SemaphoreType.DMA((count,)),
            pltpu.SemaphoreType.DMA((count,)),
        ],
        compiler_params=pltpu.CompilerParams(collective_id=0, has_side_effects=True),
    )(parts)
    return summed.reshape(value.shape)


def exchange(payload, shift, devices, place):
    perm = [(i, i ^ shift) for i in range(devices)]
    if shift == 1:
        return lax.ppermute(payload, "cell", perm)
    core = place & 1
    half = payload.shape[-2] // 2
    mine = lax.dynamic_slice_in_dim(payload, core * half, half, payload.ndim - 2)
    got = lax.ppermute(mine, "cell", perm)
    sibling = lax.ppermute(got, "cell", [(i, i ^ 1) for i in range(devices)])
    low = jnp.where(core == 0, got, sibling)
    high = jnp.where(core == 0, sibling, got)
    return jnp.concatenate([low, high], axis=payload.ndim - 2)


def body(interfaces, cell_profile, cell_section, mode_loss, phase, mode_field, target):
    mode_count = mode_loss.shape[1]
    waves_here = phase.shape[1]
    devices = lax.axis_size("cell")
    place = lax.axis_index("cell")

    selected = jnp.take(interfaces, cell_section, axis=0)[:, None]
    amplitude = jnp.take(mode_loss, cell_profile, axis=0)[:, None, :]
    angle = jnp.take(phase, cell_profile, axis=0)
    cells = build_cells(selected, amplitude * jnp.cos(angle), amplitude * jnp.sin(angle))

    unit = jnp.stack(
        [jnp.eye(mode_count, dtype=jnp.float32), jnp.zeros((mode_count, mode_count), jnp.float32)]
    )
    unit = jnp.broadcast_to(unit, (waves_here, 2, mode_count, mode_count))
    zero = jnp.zeros_like(unit)

    local_suffix = suffix_scan(cells)
    prefix_input = cells[1]
    local_incoming = None
    block = jax.tree.map(lambda a: a[0], local_suffix)

    row_count = mode_count // devices
    total = block
    right = (zero, unit, unit)
    left = unit
    shift = 1
    while shift < devices // 2:
        perm = [(i, i ^ shift) for i in range(devices)]
        payload = jnp.stack(total)
        if local_incoming is None and shift > 1:
            payload, prefix_input = lax.optimization_barrier((payload, prefix_input))
            local_prefix = prefix_scan(prefix_input)
            local_incoming = jnp.concatenate([unit[None], local_prefix[:-1]], axis=0)
        other = exchange(payload, shift, devices, place)
        other = (other[0], other[1], other[2])
        upper = (place & shift) == 0
        first = pick(upper, total, other)
        second = pick(upper, other, total)
        joined = star(
            jax.tree.map(lambda a, b: jnp.stack([a, b]), right, first),
            jax.tree.map(lambda a, b: jnp.stack([a, b]), other, second),
        )
        right = pick(upper, jax.tree.map(lambda a: a[0], joined), right)
        total = jax.tree.map(lambda a: a[1], joined)
        left = jnp.where(upper, left, cmul(left, other[1]))
        shift *= 2

    perm = [(i, i ^ shift) for i in range(devices)]
    partner = place ^ shift
    pair = 2 if shift > 1 else 1
    rows_out = lax.dynamic_slice_in_dim(total[2], (partner - (partner % pair)) * row_count, pair * row_count, 2)
    sent = jnp.concatenate([total[0], total[1], rows_out], axis=2)
    got = exchange(sent, shift, devices, place)
    other_refl = got[:, :, :mode_count]
    other_trans = got[:, :, mode_count : 2 * mode_count]
    other_rows = lax.dynamic_slice_in_dim(got, 2 * mode_count + (place % pair) * row_count, row_count, 2)
    upper = (place & shift) == 0
    own_rows = lax.dynamic_slice_in_dim(total[2], place * row_count, row_count, 2)
    first_refl = jnp.where(upper, total[0], other_refl)
    first_trans = jnp.where(upper, total[1], other_trans)
    first_rows = jnp.where(upper, own_rows, other_rows)
    second_refl = jnp.where(upper, other_refl, total[0])
    second_trans = jnp.where(upper, other_trans, total[1])
    joined = star(
        (right[0], right[1], right[2]),
        (other_refl, other_trans, None),
        need_back=False,
    )
    right = (jnp.where(upper, joined[0], right[0]), jnp.where(upper, joined[1], right[1]))
    left = jnp.where(upper, left, cmul(left, other_trans))
    total_trans = cmul(second_trans, first_trans)
    mine = lax.dynamic_slice_in_dim(first_refl, place * row_count, row_count, 2) + cmul(
        cmul(first_rows, second_refl), first_trans
    )


    if local_incoming is None:
        local_prefix = prefix_scan(prefix_input)
        local_incoming = jnp.concatenate([unit[None], local_prefix[:-1]], axis=0)

    suffix_refl = local_suffix[0] + cmul(cmul(local_suffix[2], right[0][None]), local_suffix[1])
    suffix_trans = cmul(right[1][None], local_suffix[1])
    incoming = cmul(local_incoming, left[None])

    mismatch = total_trans - target
    fields = incoming + cmul(suffix_refl, incoming)
    adjoint = cmul(jnp.swapaxes(suffix_trans, -1, -2), mismatch[None])
    coupling = jnp.einsum(
        "cwij,cwkj->cik", fields[:, :, 0], adjoint[:, :, 0], precision=HIGHEST
    ) - jnp.einsum("cwij,cwkj->cik", fields[:, :, 1], adjoint[:, :, 1], precision=HIGHEST)
    summed = wl_sum(coupling)
    chosen = jnp.take(mode_field, cell_profile, axis=0)
    weighted = jnp.einsum("cmn,cnx->cmx", summed, chosen, precision=HIGHEST)
    gradient = jnp.sum(chosen * weighted, axis=1)

    return (mine, gradient)


def solution(mesh):
    in_specs = (
        P(),
        P("cell"),
        P("cell"),
        P(),
        P(None, "wl", None),
        P(None, None, "wl"),
        P("wl", None, None, None),
    )
    out_specs = (P("wl", None, "cell", None), P("cell", "wl"))
    return jax.shard_map(body, mesh=mesh, in_specs=in_specs, out_specs=out_specs, check_vma=False)
```

```python
import functools

import jax
import jax.numpy as jnp
from jax import lax
from jax.experimental import pallas as pl
from jax.experimental.pallas import tpu as pltpu
from jax.sharding import PartitionSpec as P

HIGHEST = lax.Precision.HIGHEST


def cmul(left, right):
    parts = jnp.einsum("...pmk,...qkn->...pqmn", left, right, precision=HIGHEST)
    real = parts[..., 0, 0, :, :] - parts[..., 1, 1, :, :]
    imag = parts[..., 0, 1, :, :] + parts[..., 1, 0, :, :]
    return jnp.stack([real, imag], axis=-3)


def star(former, latter, need_back=True):
    refl_f, trans_f, back_f = former
    refl_l, trans_l, back_l = latter
    reflect = refl_f + cmul(cmul(back_f, refl_l), trans_f)
    trans = cmul(trans_l, trans_f)
    back = cmul(back_f, back_l) if need_back else None
    return (reflect, trans, back)


def pick(flag, a, b):
    return jax.tree.map(lambda u, v: jnp.where(flag, u, v), a, b)


def cat(a, b):
    return jax.tree.map(lambda u, v: jnp.concatenate([u, v], axis=0), a, b)


def interleave(even, odd):
    return jnp.stack([even, odd], axis=1).reshape((-1,) + even.shape[1:])


def suffix_scan(cells):
    count = cells[0].shape[0]
    shift = 1
    while shift < count:
        head = jax.tree.map(lambda a: a[: count - shift], cells)
        tail = jax.tree.map(lambda a: a[shift:], cells)
        joined = star(head, tail)
        cells = cat(joined, jax.tree.map(lambda a: a[count - shift :], cells))
        shift *= 2
    return cells


def suffix_scan_head(cells):
    count = cells[0].shape[0]
    shift = 1
    while shift * 2 < count:
        head = jax.tree.map(lambda a: a[: count - shift], cells)
        tail = jax.tree.map(lambda a: a[shift:], cells)
        joined = star(head, tail)
        cells = cat(joined, jax.tree.map(lambda a: a[count - shift :], cells))
        shift *= 2
    if shift >= count:
        return cells, None
    first = star(jax.tree.map(lambda a: a[:1], cells), jax.tree.map(lambda a: a[shift : shift + 1], cells))
    return cells, first


def suffix_scan_tail(cells, first):
    if first is None:
        return cells
    count = cells[0].shape[0]
    shift = count // 2
    parts = [first]
    if shift > 1:
        parts.append(star(jax.tree.map(lambda a: a[1:shift], cells), jax.tree.map(lambda a: a[shift + 1 :], cells)))
    parts.append(jax.tree.map(lambda a: a[shift:], cells))
    return jax.tree.map(lambda *a: jnp.concatenate(a, axis=0), *parts)


def prefix_scan(trans):
    count = trans.shape[0]
    shift = 1
    while shift < count:
        joined = cmul(trans[shift:], trans[: count - shift])
        trans = jnp.concatenate([trans[:shift], joined], axis=0)
        shift *= 2
    return trans


def build_cells(selected, prop_real, prop_imag):
    forward = selected[:, :, 1]
    backward = selected[:, :, 2]
    row_real = prop_real[..., :, None]
    row_imag = prop_imag[..., :, None]
    trans = jnp.stack(
        [
            row_real * forward[:, :, 0] - row_imag * forward[:, :, 1],
            row_real * forward[:, :, 1] + row_imag * forward[:, :, 0],
        ],
        axis=2,
    )
    col_real = prop_real[..., None, :]
    col_imag = prop_imag[..., None, :]
    back = jnp.stack(
        [
            backward[:, :, 0] * col_real - backward[:, :, 1] * col_imag,
            backward[:, :, 0] * col_imag + backward[:, :, 1] * col_real,
        ],
        axis=2,
    )
    reflect = jnp.broadcast_to(selected[:, :, 0], trans.shape)
    return (reflect, trans, back)


def wl_sum_kernel(count, part_ref, out_ref, held, send_a, recv_a, send_b, recv_b):
    me = lax.axis_index("wl")
    row = lax.axis_index("cell")
    mesh_id = pl.DeviceIdType.MESH

    def link(src, dst, send, recv, peer):
        return pltpu.make_async_remote_copy(
            src_ref=src, dst_ref=dst, send_sem=send, recv_sem=recv,
            device_id=(peer, row), device_id_type=mesh_id,
        )

    barrier = pltpu.get_barrier_semaphore()
    for step in range(1, count):
        peer = lax.rem(me + step, count)
        pl.semaphore_signal(barrier, inc=1, device_id=(peer, row), device_id_type=mesh_id)
    pl.semaphore_wait(barrier, count - 1)

    outgoing = []
    for step in range(1, count):
        peer = lax.rem(me + step, count)
        copy = link(part_ref.at[peer], held.at[me], send_a.at[peer], recv_a.at[me], peer)
        copy.start()
        outgoing.append(copy)
    total = part_ref[me]
    for step in range(1, count):
        source = lax.rem(me + count - step, count)
        link(part_ref.at[source], held.at[source], send_a.at[source], recv_a.at[source], source).wait_recv()
        total = total + held[source]
    out_ref[me] = total
    for copy in outgoing:
        copy.wait_send()

    outgoing = []
    for step in range(1, count):
        peer = lax.rem(me + step, count)
        copy = link(out_ref.at[me], out_ref.at[me], send_b.at[peer], recv_b.at[me], peer)
        copy.start()
        outgoing.append(copy)
    for step in range(1, count):
        source = lax.rem(me + count - step, count)
        link(out_ref.at[source], out_ref.at[source], send_b.at[source], recv_b.at[source], source).wait_recv()
    for copy in outgoing:
        copy.wait_send()


def wl_sum(value):
    count = lax.axis_size("wl")
    lanes = value.shape[-1]
    parts = value.reshape(count, -1, lanes)
    summed = pl.pallas_call(
        functools.partial(wl_sum_kernel, count),
        out_shape=jax.ShapeDtypeStruct(parts.shape, parts.dtype),
        in_specs=[pl.BlockSpec(memory_space=pltpu.VMEM)],
        out_specs=pl.BlockSpec(memory_space=pltpu.VMEM),
        scratch_shapes=[
            pltpu.VMEM(parts.shape, parts.dtype),
            pltpu.SemaphoreType.DMA((count,)),
            pltpu.SemaphoreType.DMA((count,)),
            pltpu.SemaphoreType.DMA((count,)),
            pltpu.SemaphoreType.DMA((count,)),
        ],
        compiler_params=pltpu.CompilerParams(collective_id=0, has_side_effects=True),
    )(parts)
    return summed.reshape(value.shape)


def exchange(payload, shift, devices, place):
    perm = [(i, i ^ shift) for i in range(devices)]
    if shift == 1:
        return lax.ppermute(payload, "cell", perm)
    core = place & 1
    half = payload.shape[-2] // 2
    mine = lax.dynamic_slice_in_dim(payload, core * half, half, payload.ndim - 2)
    got = lax.ppermute(mine, "cell", perm)
    sibling = lax.ppermute(got, "cell", [(i, i ^ 1) for i in range(devices)])
    low = jnp.where(core == 0, got, sibling)
    high = jnp.where(core == 0, sibling, got)
    return jnp.concatenate([low, high], axis=payload.ndim - 2)


def body(interfaces, cell_profile, cell_section, mode_loss, phase, mode_field, target):
    mode_count = mode_loss.shape[1]
    waves_here = phase.shape[1]
    devices = lax.axis_size("cell")
    place = lax.axis_index("cell")

    selected = jnp.take(interfaces, cell_section, axis=0)[:, None]
    amplitude = jnp.take(mode_loss, cell_profile, axis=0)[:, None, :]
    angle = jnp.take(phase, cell_profile, axis=0)
    cells = build_cells(selected, amplitude * jnp.cos(angle), amplitude * jnp.sin(angle))

    unit = jnp.stack(
        [jnp.eye(mode_count, dtype=jnp.float32), jnp.zeros((mode_count, mode_count), jnp.float32)]
    )
    unit = jnp.broadcast_to(unit, (waves_here, 2, mode_count, mode_count))
    zero = jnp.zeros_like(unit)

    scanned, lead = suffix_scan_head(cells)
    local_suffix = None
    prefix_input = cells[1]
    local_incoming = None
    block = jax.tree.map(lambda a: a[0], lead if lead is not None else scanned)

    row_count = mode_count // devices
    total = block
    right = (zero, unit, unit)
    left = unit
    shift = 1
    while shift < devices // 2:
        perm = [(i, i ^ shift) for i in range(devices)]
        payload = jnp.stack(total)
        if local_incoming is None and shift > 1:
            payload, prefix_input = lax.optimization_barrier((payload, prefix_input))
            local_prefix = prefix_scan(prefix_input)
            local_incoming = jnp.concatenate([unit[None], local_prefix[:-1]], axis=0)
        elif local_suffix is None and shift > 2:
            payload, (scanned, lead) = lax.optimization_barrier((payload, (scanned, lead)))
            local_suffix = suffix_scan_tail(scanned, lead)
        other = exchange(payload, shift, devices, place)
        other = (other[0], other[1], other[2])
        upper = (place & shift) == 0
        first = pick(upper, total, other)
        second = pick(upper, other, total)
        joined = star(
            jax.tree.map(lambda a, b: jnp.stack([a, b]), right, first),
            jax.tree.map(lambda a, b: jnp.stack([a, b]), other, second),
        )
        right = pick(upper, jax.tree.map(lambda a: a[0], joined), right)
        total = jax.tree.map(lambda a: a[1], joined)
        left = jnp.where(upper, left, cmul(left, other[1]))
        shift *= 2

    perm = [(i, i ^ shift) for i in range(devices)]
    partner = place ^ shift
    pair = 2 if shift > 1 else 1
    rows_out = lax.dynamic_slice_in_dim(total[2], (partner - (partner % pair)) * row_count, pair * row_count, 2)
    sent = jnp.concatenate([total[0], total[1], rows_out], axis=2)
    got = exchange(sent, shift, devices, place)
    other_refl = got[:, :, :mode_count]
    other_trans = got[:, :, mode_count : 2 * mode_count]
    other_rows = lax.dynamic_slice_in_dim(got, 2 * mode_count + (place % pair) * row_count, row_count, 2)
    upper = (place & shift) == 0
    own_rows = lax.dynamic_slice_in_dim(total[2], place * row_count, row_count, 2)
    first_refl = jnp.where(upper, total[0], other_refl)
    first_trans = jnp.where(upper, total[1], other_trans)
    first_rows = jnp.where(upper, own_rows, other_rows)
    second_refl = jnp.where(upper, other_refl, total[0])
    second_trans = jnp.where(upper, other_trans, total[1])
    joined = star(
        (right[0], right[1], right[2]),
        (other_refl, other_trans, None),
        need_back=False,
    )
    right = (jnp.where(upper, joined[0], right[0]), jnp.where(upper, joined[1], right[1]))
    left = jnp.where(upper, left, cmul(left, other_trans))
    total_trans = cmul(second_trans, first_trans)
    mine = lax.dynamic_slice_in_dim(first_refl, place * row_count, row_count, 2) + cmul(
        cmul(first_rows, second_refl), first_trans
    )


    if local_suffix is None:
        local_suffix = suffix_scan_tail(scanned, lead)
    if local_incoming is None:
        local_prefix = prefix_scan(prefix_input)
        local_incoming = jnp.concatenate([unit[None], local_prefix[:-1]], axis=0)

    suffix_refl = local_suffix[0] + cmul(cmul(local_suffix[2], right[0][None]), local_suffix[1])
    suffix_trans = cmul(right[1][None], local_suffix[1])
    incoming = cmul(local_incoming, left[None])

    mismatch = total_trans - target
    fields = incoming + cmul(suffix_refl, incoming)
    adjoint = cmul(jnp.swapaxes(suffix_trans, -1, -2), mismatch[None])
    coupling = jnp.einsum(
        "cwij,cwkj->cik", fields[:, :, 0], adjoint[:, :, 0], precision=HIGHEST
    ) - jnp.einsum("cwij,cwkj->cik", fields[:, :, 1], adjoint[:, :, 1], precision=HIGHEST)
    summed = wl_sum(coupling)
    chosen = jnp.take(mode_field, cell_profile, axis=0)
    weighted = jnp.einsum("cmn,cnx->cmx", summed, chosen, precision=HIGHEST)
    gradient = jnp.sum(chosen * weighted, axis=1)

    return (mine, gradient)


def solution(mesh):
    in_specs = (
        P(),
        P("cell"),
        P("cell"),
        P(),
        P(None, "wl", None),
        P(None, None, "wl"),
        P("wl", None, None, None),
    )
    out_specs = (P("wl", None, "cell", None), P("cell", "wl"))
    return jax.shard_map(body, mesh=mesh, in_specs=in_specs, out_specs=out_specs, check_vma=False)
```

```python
import functools

import jax
import jax.numpy as jnp
from jax import lax
from jax.experimental import pallas as pl
from jax.experimental.pallas import tpu as pltpu
from jax.sharding import PartitionSpec as P

HIGHEST = lax.Precision.HIGHEST


def cmul(left, right):
    parts = jnp.einsum("...pmk,...qkn->...pqmn", left, right, precision=HIGHEST)
    real = parts[..., 0, 0, :, :] - parts[..., 1, 1, :, :]
    imag = parts[..., 0, 1, :, :] + parts[..., 1, 0, :, :]
    return jnp.stack([real, imag], axis=-3)


def star(former, latter, need_back=True):
    refl_f, trans_f, back_f = former
    refl_l, trans_l, back_l = latter
    reflect = refl_f + cmul(cmul(back_f, refl_l), trans_f)
    trans = cmul(trans_l, trans_f)
    back = cmul(back_f, back_l) if need_back else None
    return (reflect, trans, back)


def pick(flag, a, b):
    return jax.tree.map(lambda u, v: jnp.where(flag, u, v), a, b)


def cat(a, b):
    return jax.tree.map(lambda u, v: jnp.concatenate([u, v], axis=0), a, b)


def interleave(even, odd):
    return jnp.stack([even, odd], axis=1).reshape((-1,) + even.shape[1:])


def suffix_scan(cells):
    count = cells[0].shape[0]
    shift = 1
    while shift < count:
        head = jax.tree.map(lambda a: a[: count - shift], cells)
        tail = jax.tree.map(lambda a: a[shift:], cells)
        joined = star(head, tail)
        cells = cat(joined, jax.tree.map(lambda a: a[count - shift :], cells))
        shift *= 2
    return cells


def prefix_scan(trans):
    count = trans.shape[0]
    shift = 1
    while shift < count:
        joined = cmul(trans[shift:], trans[: count - shift])
        trans = jnp.concatenate([trans[:shift], joined], axis=0)
        shift *= 2
    return trans


def build_cells(selected, prop_real, prop_imag):
    forward = selected[:, :, 1]
    backward = selected[:, :, 2]
    row_real = prop_real[..., :, None]
    row_imag = prop_imag[..., :, None]
    trans = jnp.stack(
        [
            row_real * forward[:, :, 0] - row_imag * forward[:, :, 1],
            row_real * forward[:, :, 1] + row_imag * forward[:, :, 0],
        ],
        axis=2,
    )
    col_real = prop_real[..., None, :]
    col_imag = prop_imag[..., None, :]
    back = jnp.stack(
        [
            backward[:, :, 0] * col_real - backward[:, :, 1] * col_imag,
            backward[:, :, 0] * col_imag + backward[:, :, 1] * col_real,
        ],
        axis=2,
    )
    reflect = jnp.broadcast_to(selected[:, :, 0], trans.shape)
    return (reflect, trans, back)


def wl_sum_kernel(count, part_ref, out_ref, held, send_a, recv_a, send_b, recv_b):
    me = lax.axis_index("wl")
    row = lax.axis_index("cell")
    mesh_id = pl.DeviceIdType.MESH

    def link(src, dst, send, recv, peer):
        return pltpu.make_async_remote_copy(
            src_ref=src, dst_ref=dst, send_sem=send, recv_sem=recv,
            device_id=(peer, row), device_id_type=mesh_id,
        )

    barrier = pltpu.get_barrier_semaphore()
    for step in range(1, count):
        peer = lax.rem(me + step, count)
        pl.semaphore_signal(barrier, inc=1, device_id=(peer, row), device_id_type=mesh_id)
    pl.semaphore_wait(barrier, count - 1)

    outgoing = []
    for step in range(1, count):
        peer = lax.rem(me + step, count)
        copy = link(part_ref.at[peer], held.at[me], send_a.at[peer], recv_a.at[me], peer)
        copy.start()
        outgoing.append(copy)
    total = part_ref[me]
    for step in range(1, count):
        source = lax.rem(me + count - step, count)
        link(part_ref.at[source], held.at[source], send_a.at[source], recv_a.at[source], source).wait_recv()
        total = total + held[source]
    out_ref[me] = total
    for copy in outgoing:
        copy.wait_send()

    outgoing = []
    for step in range(1, count):
        peer = lax.rem(me + step, count)
        copy = link(out_ref.at[me], out_ref.at[me], send_b.at[peer], recv_b.at[me], peer)
        copy.start()
        outgoing.append(copy)
    for step in range(1, count):
        source = lax.rem(me + count - step, count)
        link(out_ref.at[source], out_ref.at[source], send_b.at[source], recv_b.at[source], source).wait_recv()
    for copy in outgoing:
        copy.wait_send()


def wl_sum(value):
    count = lax.axis_size("wl")
    lanes = value.shape[-1]
    parts = value.reshape(count, -1, lanes)
    summed = pl.pallas_call(
        functools.partial(wl_sum_kernel, count),
        out_shape=jax.ShapeDtypeStruct(parts.shape, parts.dtype),
        in_specs=[pl.BlockSpec(memory_space=pltpu.VMEM)],
        out_specs=pl.BlockSpec(memory_space=pltpu.VMEM),
        scratch_shapes=[
            pltpu.VMEM(parts.shape, parts.dtype),
            pltpu.SemaphoreType.DMA((count,)),
            pltpu.SemaphoreType.DMA((count,)),
            pltpu.SemaphoreType.DMA((count,)),
            pltpu.SemaphoreType.DMA((count,)),
        ],
        compiler_params=pltpu.CompilerParams(collective_id=0, has_side_effects=True),
    )(parts)
    return summed.reshape(value.shape)


def exchange(payload, shift, devices, place):
    perm = [(i, i ^ shift) for i in range(devices)]
    if shift == 1:
        return lax.ppermute(payload, "cell", perm)
    core = place & 1
    half = payload.shape[-2] // 2
    mine = lax.dynamic_slice_in_dim(payload, core * half, half, payload.ndim - 2)
    got = lax.ppermute(mine, "cell", perm)
    sibling = lax.ppermute(got, "cell", [(i, i ^ 1) for i in range(devices)])
    low = jnp.where(core == 0, got, sibling)
    high = jnp.where(core == 0, sibling, got)
    return jnp.concatenate([low, high], axis=payload.ndim - 2)


def body(interfaces, cell_profile, cell_section, mode_loss, phase, mode_field, target):
    mode_count = mode_loss.shape[1]
    waves_here = phase.shape[1]
    devices = lax.axis_size("cell")
    place = lax.axis_index("cell")

    selected = jnp.take(interfaces, cell_section, axis=0)[:, None]
    amplitude = jnp.take(mode_loss, cell_profile, axis=0)[:, None, :]
    angle = jnp.take(phase, cell_profile, axis=0)
    cells = build_cells(selected, amplitude * jnp.cos(angle), amplitude * jnp.sin(angle))

    unit = jnp.stack(
        [jnp.eye(mode_count, dtype=jnp.float32), jnp.zeros((mode_count, mode_count), jnp.float32)]
    )
    unit = jnp.broadcast_to(unit, (waves_here, 2, mode_count, mode_count))
    zero = jnp.zeros_like(unit)

    local_suffix = suffix_scan(cells)
    prefix_input = cells[1]
    local_incoming = None
    block = jax.tree.map(lambda a: a[0], local_suffix)

    row_count = mode_count // devices
    total = block
    right = (zero, unit, unit)
    left = unit
    shift = 1
    while shift < devices // 2:
        perm = [(i, i ^ shift) for i in range(devices)]
        payload = jnp.stack(total)
        if local_incoming is None and shift > 2:
            payload, prefix_input = lax.optimization_barrier((payload, prefix_input))
            local_prefix = prefix_scan(prefix_input)
            local_incoming = jnp.concatenate([unit[None], local_prefix[:-1]], axis=0)
        other = exchange(payload, shift, devices, place)
        other = (other[0], other[1], other[2])
        upper = (place & shift) == 0
        first = pick(upper, total, other)
        second = pick(upper, other, total)
        joined = star(
            jax.tree.map(lambda a, b: jnp.stack([a, b]), right, first),
            jax.tree.map(lambda a, b: jnp.stack([a, b]), other, second),
        )
        right = pick(upper, jax.tree.map(lambda a: a[0], joined), right)
        total = jax.tree.map(lambda a: a[1], joined)
        left = jnp.where(upper, left, cmul(left, other[1]))
        shift *= 2

    perm = [(i, i ^ shift) for i in range(devices)]
    partner = place ^ shift
    pair = 2 if shift > 1 else 1
    rows_out = lax.dynamic_slice_in_dim(total[2], (partner - (partner % pair)) * row_count, pair * row_count, 2)
    sent = jnp.concatenate([total[0], total[1], rows_out], axis=2)
    got = exchange(sent, shift, devices, place)
    other_refl = got[:, :, :mode_count]
    other_trans = got[:, :, mode_count : 2 * mode_count]
    other_rows = lax.dynamic_slice_in_dim(got, 2 * mode_count + (place % pair) * row_count, row_count, 2)
    upper = (place & shift) == 0
    own_rows = lax.dynamic_slice_in_dim(total[2], place * row_count, row_count, 2)
    first_refl = jnp.where(upper, total[0], other_refl)
    first_trans = jnp.where(upper, total[1], other_trans)
    first_rows = jnp.where(upper, own_rows, other_rows)
    second_refl = jnp.where(upper, other_refl, total[0])
    second_trans = jnp.where(upper, other_trans, total[1])
    joined = star(
        (right[0], right[1], right[2]),
        (other_refl, other_trans, None),
        need_back=False,
    )
    right = (jnp.where(upper, joined[0], right[0]), jnp.where(upper, joined[1], right[1]))
    left = jnp.where(upper, left, cmul(left, other_trans))
    total_trans = cmul(second_trans, first_trans)
    mine = lax.dynamic_slice_in_dim(first_refl, place * row_count, row_count, 2) + cmul(
        cmul(first_rows, second_refl), first_trans
    )


    if local_incoming is None:
        local_prefix = prefix_scan(prefix_input)
        local_incoming = jnp.concatenate([unit[None], local_prefix[:-1]], axis=0)

    suffix_refl = local_suffix[0] + cmul(cmul(local_suffix[2], right[0][None]), local_suffix[1])
    suffix_trans = cmul(right[1][None], local_suffix[1])
    incoming = cmul(local_incoming, left[None])

    mismatch = total_trans - target
    fields = incoming + cmul(suffix_refl, incoming)
    adjoint = cmul(jnp.swapaxes(suffix_trans, -1, -2), mismatch[None])
    coupling = jnp.einsum(
        "cwij,cwkj->cik", fields[:, :, 0], adjoint[:, :, 0], precision=HIGHEST
    ) - jnp.einsum("cwij,cwkj->cik", fields[:, :, 1], adjoint[:, :, 1], precision=HIGHEST)
    summed = wl_sum(coupling)
    chosen = jnp.take(mode_field, cell_profile, axis=0)
    weighted = jnp.einsum("cmn,cnx->cmx", summed, chosen, precision=HIGHEST)
    gradient = jnp.sum(chosen * weighted, axis=1)

    return (mine, gradient)


def solution(mesh):
    in_specs = (
        P(),
        P("cell"),
        P("cell"),
        P(),
        P(None, "wl", None),
        P(None, None, "wl"),
        P("wl", None, None, None),
    )
    out_specs = (P("wl", None, "cell", None), P("cell", "wl"))
    return jax.shard_map(body, mesh=mesh, in_specs=in_specs, out_specs=out_specs, check_vma=False)
```

```python
import functools

import jax
import jax.numpy as jnp
from jax import lax
from jax.experimental import pallas as pl
from jax.experimental.pallas import tpu as pltpu
from jax.sharding import PartitionSpec as P

HIGHEST = lax.Precision.HIGHEST


def cmul(left, right):
    parts = jnp.einsum("...pmk,...qkn->...pqmn", left, right, precision=HIGHEST)
    real = parts[..., 0, 0, :, :] - parts[..., 1, 1, :, :]
    imag = parts[..., 0, 1, :, :] + parts[..., 1, 0, :, :]
    return jnp.stack([real, imag], axis=-3)


def star(former, latter, need_back=True):
    refl_f, trans_f, back_f = former
    refl_l, trans_l, back_l = latter
    reflect = refl_f + cmul(cmul(back_f, refl_l), trans_f)
    trans = cmul(trans_l, trans_f)
    back = cmul(back_f, back_l) if need_back else None
    return (reflect, trans, back)


def pick(flag, a, b):
    return jax.tree.map(lambda u, v: jnp.where(flag, u, v), a, b)


def cat(a, b):
    return jax.tree.map(lambda u, v: jnp.concatenate([u, v], axis=0), a, b)


def interleave(even, odd):
    return jnp.stack([even, odd], axis=1).reshape((-1,) + even.shape[1:])


def suffix_scan(cells):
    count = cells[0].shape[0]
    shift = 1
    while shift < count:
        head = jax.tree.map(lambda a: a[: count - shift], cells)
        tail = jax.tree.map(lambda a: a[shift:], cells)
        joined = star(head, tail)
        cells = cat(joined, jax.tree.map(lambda a: a[count - shift :], cells))
        shift *= 2
    return cells


def suffix_scan_head(cells):
    count = cells[0].shape[0]
    shift = 1
    while shift * 2 < count:
        head = jax.tree.map(lambda a: a[: count - shift], cells)
        tail = jax.tree.map(lambda a: a[shift:], cells)
        joined = star(head, tail)
        cells = cat(joined, jax.tree.map(lambda a: a[count - shift :], cells))
        shift *= 2
    if shift >= count:
        return cells, None
    first = star(jax.tree.map(lambda a: a[:1], cells), jax.tree.map(lambda a: a[shift : shift + 1], cells))
    return cells, first


def suffix_scan_tail(cells, first):
    if first is None:
        return cells
    count = cells[0].shape[0]
    shift = count // 2
    parts = [first]
    if shift > 1:
        parts.append(star(jax.tree.map(lambda a: a[1:shift], cells), jax.tree.map(lambda a: a[shift + 1 :], cells)))
    parts.append(jax.tree.map(lambda a: a[shift:], cells))
    return jax.tree.map(lambda *a: jnp.concatenate(a, axis=0), *parts)


def prefix_scan(trans):
    count = trans.shape[0]
    shift = 1
    while shift < count:
        joined = cmul(trans[shift:], trans[: count - shift])
        trans = jnp.concatenate([trans[:shift], joined], axis=0)
        shift *= 2
    return trans


def build_cells(selected, prop_real, prop_imag):
    forward = selected[:, :, 1]
    backward = selected[:, :, 2]
    row_real = prop_real[..., :, None]
    row_imag = prop_imag[..., :, None]
    trans = jnp.stack(
        [
            row_real * forward[:, :, 0] - row_imag * forward[:, :, 1],
            row_real * forward[:, :, 1] + row_imag * forward[:, :, 0],
        ],
        axis=2,
    )
    col_real = prop_real[..., None, :]
    col_imag = prop_imag[..., None, :]
    back = jnp.stack(
        [
            backward[:, :, 0] * col_real - backward[:, :, 1] * col_imag,
            backward[:, :, 0] * col_imag + backward[:, :, 1] * col_real,
        ],
        axis=2,
    )
    reflect = jnp.broadcast_to(selected[:, :, 0], trans.shape)
    return (reflect, trans, back)


def wl_sum_kernel(count, part_ref, out_ref, held, send_a, recv_a, send_b, recv_b):
    me = lax.axis_index("wl")
    row = lax.axis_index("cell")
    mesh_id = pl.DeviceIdType.MESH

    def link(src, dst, send, recv, peer):
        return pltpu.make_async_remote_copy(
            src_ref=src, dst_ref=dst, send_sem=send, recv_sem=recv,
            device_id=(peer, row), device_id_type=mesh_id,
        )

    barrier = pltpu.get_barrier_semaphore()
    for step in range(1, count):
        peer = lax.rem(me + step, count)
        pl.semaphore_signal(barrier, inc=1, device_id=(peer, row), device_id_type=mesh_id)
    pl.semaphore_wait(barrier, count - 1)

    outgoing = []
    for step in range(1, count):
        peer = lax.rem(me + step, count)
        copy = link(part_ref.at[peer], held.at[me], send_a.at[peer], recv_a.at[me], peer)
        copy.start()
        outgoing.append(copy)
    total = part_ref[me]
    for step in range(1, count):
        source = lax.rem(me + count - step, count)
        link(part_ref.at[source], held.at[source], send_a.at[source], recv_a.at[source], source).wait_recv()
        total = total + held[source]
    out_ref[me] = total
    for copy in outgoing:
        copy.wait_send()

    outgoing = []
    for step in range(1, count):
        peer = lax.rem(me + step, count)
        copy = link(out_ref.at[me], out_ref.at[me], send_b.at[peer], recv_b.at[me], peer)
        copy.start()
        outgoing.append(copy)
    for step in range(1, count):
        source = lax.rem(me + count - step, count)
        link(out_ref.at[source], out_ref.at[source], send_b.at[source], recv_b.at[source], source).wait_recv()
    for copy in outgoing:
        copy.wait_send()


def wl_sum(value):
    count = lax.axis_size("wl")
    lanes = value.shape[-1]
    parts = value.reshape(count, -1, lanes)
    summed = pl.pallas_call(
        functools.partial(wl_sum_kernel, count),
        out_shape=jax.ShapeDtypeStruct(parts.shape, parts.dtype),
        in_specs=[pl.BlockSpec(memory_space=pltpu.VMEM)],
        out_specs=pl.BlockSpec(memory_space=pltpu.VMEM),
        scratch_shapes=[
            pltpu.VMEM(parts.shape, parts.dtype),
            pltpu.SemaphoreType.DMA((count,)),
            pltpu.SemaphoreType.DMA((count,)),
            pltpu.SemaphoreType.DMA((count,)),
            pltpu.SemaphoreType.DMA((count,)),
        ],
        compiler_params=pltpu.CompilerParams(collective_id=0, has_side_effects=True),
    )(parts)
    return summed.reshape(value.shape)


def exchange(payload, shift, devices, place):
    perm = [(i, i ^ shift) for i in range(devices)]
    if shift == 1:
        return lax.ppermute(payload, "cell", perm)
    core = place & 1
    half = payload.shape[-2] // 2
    mine = lax.dynamic_slice_in_dim(payload, core * half, half, payload.ndim - 2)
    got = lax.ppermute(mine, "cell", perm)
    sibling = lax.ppermute(got, "cell", [(i, i ^ 1) for i in range(devices)])
    low = jnp.where(core == 0, got, sibling)
    high = jnp.where(core == 0, sibling, got)
    return jnp.concatenate([low, high], axis=payload.ndim - 2)


def body(interfaces, cell_profile, cell_section, mode_loss, phase, mode_field, target):
    mode_count = mode_loss.shape[1]
    waves_here = phase.shape[1]
    devices = lax.axis_size("cell")
    place = lax.axis_index("cell")

    selected = jnp.take(interfaces, cell_section, axis=0)[:, None]
    amplitude = jnp.take(mode_loss, cell_profile, axis=0)[:, None, :]
    angle = jnp.take(phase, cell_profile, axis=0)
    cells = build_cells(selected, amplitude * jnp.cos(angle), amplitude * jnp.sin(angle))

    unit = jnp.stack(
        [jnp.eye(mode_count, dtype=jnp.float32), jnp.zeros((mode_count, mode_count), jnp.float32)]
    )
    unit = jnp.broadcast_to(unit, (waves_here, 2, mode_count, mode_count))
    zero = jnp.zeros_like(unit)

    scanned, lead = suffix_scan_head(cells)
    local_suffix = None
    prefix_input = cells[1]
    local_incoming = None
    block = jax.tree.map(lambda a: a[0], lead if lead is not None else scanned)

    row_count = mode_count // devices
    total = block
    right = (zero, unit, unit)
    left = unit
    shift = 1
    while shift < devices // 2:
        perm = [(i, i ^ shift) for i in range(devices)]
        payload = jnp.stack(total)
        if local_incoming is None and shift > 1:
            payload, prefix_input = lax.optimization_barrier((payload, prefix_input))
            local_prefix = prefix_scan(prefix_input)
            local_incoming = jnp.concatenate([unit[None], local_prefix[:-1]], axis=0)
        if local_suffix is None and shift > 1:
            payload, (scanned, lead) = lax.optimization_barrier((payload, (scanned, lead)))
            local_suffix = suffix_scan_tail(scanned, lead)
        other = exchange(payload, shift, devices, place)
        other = (other[0], other[1], other[2])
        upper = (place & shift) == 0
        first = pick(upper, total, other)
        second = pick(upper, other, total)
        joined = star(
            jax.tree.map(lambda a, b: jnp.stack([a, b]), right, first),
            jax.tree.map(lambda a, b: jnp.stack([a, b]), other, second),
        )
        right = pick(upper, jax.tree.map(lambda a: a[0], joined), right)
        total = jax.tree.map(lambda a: a[1], joined)
        left = jnp.where(upper, left, cmul(left, other[1]))
        shift *= 2

    perm = [(i, i ^ shift) for i in range(devices)]
    partner = place ^ shift
    pair = 2 if shift > 1 else 1
    rows_out = lax.dynamic_slice_in_dim(total[2], (partner - (partner % pair)) * row_count, pair * row_count, 2)
    sent = jnp.concatenate([total[0], total[1], rows_out], axis=2)
    got = exchange(sent, shift, devices, place)
    other_refl = got[:, :, :mode_count]
    other_trans = got[:, :, mode_count : 2 * mode_count]
    other_rows = lax.dynamic_slice_in_dim(got, 2 * mode_count + (place % pair) * row_count, row_count, 2)
    upper = (place & shift) == 0
    own_rows = lax.dynamic_slice_in_dim(total[2], place * row_count, row_count, 2)
    first_refl = jnp.where(upper, total[0], other_refl)
    first_trans = jnp.where(upper, total[1], other_trans)
    first_rows = jnp.where(upper, own_rows, other_rows)
    second_refl = jnp.where(upper, other_refl, total[0])
    second_trans = jnp.where(upper, other_trans, total[1])
    joined = star(
        (right[0], right[1], right[2]),
        (other_refl, other_trans, None),
        need_back=False,
    )
    right = (jnp.where(upper, joined[0], right[0]), jnp.where(upper, joined[1], right[1]))
    left = jnp.where(upper, left, cmul(left, other_trans))
    total_trans = cmul(second_trans, first_trans)
    mine = lax.dynamic_slice_in_dim(first_refl, place * row_count, row_count, 2) + cmul(
        cmul(first_rows, second_refl), first_trans
    )


    if local_suffix is None:
        local_suffix = suffix_scan_tail(scanned, lead)
    if local_incoming is None:
        local_prefix = prefix_scan(prefix_input)
        local_incoming = jnp.concatenate([unit[None], local_prefix[:-1]], axis=0)

    suffix_refl = local_suffix[0] + cmul(cmul(local_suffix[2], right[0][None]), local_suffix[1])
    suffix_trans = cmul(right[1][None], local_suffix[1])
    incoming = cmul(local_incoming, left[None])

    mismatch = total_trans - target
    fields = incoming + cmul(suffix_refl, incoming)
    adjoint = cmul(jnp.swapaxes(suffix_trans, -1, -2), mismatch[None])
    coupling = jnp.einsum(
        "cwij,cwkj->cik", fields[:, :, 0], adjoint[:, :, 0], precision=HIGHEST
    ) - jnp.einsum("cwij,cwkj->cik", fields[:, :, 1], adjoint[:, :, 1], precision=HIGHEST)
    summed = wl_sum(coupling)
    chosen = jnp.take(mode_field, cell_profile, axis=0)
    weighted = jnp.einsum("cmn,cnx->cmx", summed, chosen, precision=HIGHEST)
    gradient = jnp.sum(chosen * weighted, axis=1)

    return (mine, gradient)


def solution(mesh):
    in_specs = (
        P(),
        P("cell"),
        P("cell"),
        P(),
        P(None, "wl", None),
        P(None, None, "wl"),
        P("wl", None, None, None),
    )
    out_specs = (P("wl", None, "cell", None), P("cell", "wl"))
    return jax.shard_map(body, mesh=mesh, in_specs=in_specs, out_specs=out_specs, check_vma=False)
```

```python
import functools

import jax
import jax.numpy as jnp
from jax import lax
from jax.experimental import pallas as pl
from jax.experimental.pallas import tpu as pltpu
from jax.sharding import PartitionSpec as P

HIGHEST = lax.Precision.HIGHEST


def cmul(left, right):
    parts = jnp.einsum("...pmk,...qkn->...pqmn", left, right, precision=HIGHEST)
    real = parts[..., 0, 0, :, :] - parts[..., 1, 1, :, :]
    imag = parts[..., 0, 1, :, :] + parts[..., 1, 0, :, :]
    return jnp.stack([real, imag], axis=-3)


def star(former, latter, need_back=True):
    refl_f, trans_f, back_f = former
    refl_l, trans_l, back_l = latter
    reflect = refl_f + cmul(cmul(back_f, refl_l), trans_f)
    trans = cmul(trans_l, trans_f)
    back = cmul(back_f, back_l) if need_back else None
    return (reflect, trans, back)


def pick(flag, a, b):
    return jax.tree.map(lambda u, v: jnp.where(flag, u, v), a, b)


def cat(a, b):
    return jax.tree.map(lambda u, v: jnp.concatenate([u, v], axis=0), a, b)


def interleave(even, odd):
    return jnp.stack([even, odd], axis=1).reshape((-1,) + even.shape[1:])


def suffix_scan(cells):
    count = cells[0].shape[0]
    shift = 1
    while shift < count:
        head = jax.tree.map(lambda a: a[: count - shift], cells)
        tail = jax.tree.map(lambda a: a[shift:], cells)
        joined = star(head, tail)
        cells = cat(joined, jax.tree.map(lambda a: a[count - shift :], cells))
        shift *= 2
    return cells


def prefix_scan(trans):
    count = trans.shape[0]
    shift = 1
    while shift < count:
        joined = cmul(trans[shift:], trans[: count - shift])
        trans = jnp.concatenate([trans[:shift], joined], axis=0)
        shift *= 2
    return trans


def build_cells(selected, prop_real, prop_imag):
    forward = selected[:, :, 1]
    backward = selected[:, :, 2]
    row_real = prop_real[..., :, None]
    row_imag = prop_imag[..., :, None]
    trans = jnp.stack(
        [
            row_real * forward[:, :, 0] - row_imag * forward[:, :, 1],
            row_real * forward[:, :, 1] + row_imag * forward[:, :, 0],
        ],
        axis=2,
    )
    col_real = prop_real[..., None, :]
    col_imag = prop_imag[..., None, :]
    back = jnp.stack(
        [
            backward[:, :, 0] * col_real - backward[:, :, 1] * col_imag,
            backward[:, :, 0] * col_imag + backward[:, :, 1] * col_real,
        ],
        axis=2,
    )
    reflect = jnp.broadcast_to(selected[:, :, 0], trans.shape)
    return (reflect, trans, back)


def wl_sum_kernel(count, part_ref, out_ref, held, send_a, recv_a, send_b, recv_b):
    me = lax.axis_index("wl")
    row = lax.axis_index("cell")
    mesh_id = pl.DeviceIdType.MESH

    def link(src, dst, send, recv, peer):
        return pltpu.make_async_remote_copy(
            src_ref=src, dst_ref=dst, send_sem=send, recv_sem=recv,
            device_id=(peer, row), device_id_type=mesh_id,
        )

    barrier = pltpu.get_barrier_semaphore()
    for step in range(1, count):
        peer = lax.rem(me + step, count)
        pl.semaphore_signal(barrier, inc=1, device_id=(peer, row), device_id_type=mesh_id)
    pl.semaphore_wait(barrier, count - 1)

    outgoing = []
    for step in range(1, count):
        peer = lax.rem(me + step, count)
        copy = link(part_ref.at[peer], held.at[me], send_a.at[peer], recv_a.at[me], peer)
        copy.start()
        outgoing.append(copy)
    total = part_ref[me]
    for step in range(1, count):
        source = lax.rem(me + count - step, count)
        link(part_ref.at[source], held.at[source], send_a.at[source], recv_a.at[source], source).wait_recv()
        total = total + held[source]
    out_ref[me] = total
    for copy in outgoing:
        copy.wait_send()

    outgoing = []
    for step in range(1, count):
        peer = lax.rem(me + step, count)
        copy = link(out_ref.at[me], out_ref.at[me], send_b.at[peer], recv_b.at[me], peer)
        copy.start()
        outgoing.append(copy)
    for step in range(1, count):
        source = lax.rem(me + count - step, count)
        link(out_ref.at[source], out_ref.at[source], send_b.at[source], recv_b.at[source], source).wait_recv()
    for copy in outgoing:
        copy.wait_send()


def wl_sum(value):
    count = lax.axis_size("wl")
    lanes = value.shape[-1]
    parts = value.reshape(count, -1, lanes)
    summed = pl.pallas_call(
        functools.partial(wl_sum_kernel, count),
        out_shape=jax.ShapeDtypeStruct(parts.shape, parts.dtype),
        in_specs=[pl.BlockSpec(memory_space=pltpu.VMEM)],
        out_specs=pl.BlockSpec(memory_space=pltpu.VMEM),
        scratch_shapes=[
            pltpu.VMEM(parts.shape, parts.dtype),
            pltpu.SemaphoreType.DMA((count,)),
            pltpu.SemaphoreType.DMA((count,)),
            pltpu.SemaphoreType.DMA((count,)),
            pltpu.SemaphoreType.DMA((count,)),
        ],
        compiler_params=pltpu.CompilerParams(collective_id=0, has_side_effects=True),
    )(parts)
    return summed.reshape(value.shape)


def exchange(payload, shift, devices, place):
    perm = [(i, i ^ shift) for i in range(devices)]
    if shift == 1:
        return lax.ppermute(payload, "cell", perm)
    core = place & 1
    half = payload.shape[-2] // 2
    mine = lax.dynamic_slice_in_dim(payload, core * half, half, payload.ndim - 2)
    got = lax.ppermute(mine, "cell", perm)
    sibling = lax.ppermute(got, "cell", [(i, i ^ 1) for i in range(devices)])
    low = jnp.where(core == 0, got, sibling)
    high = jnp.where(core == 0, sibling, got)
    return jnp.concatenate([low, high], axis=payload.ndim - 2)


def body(interfaces, cell_profile, cell_section, mode_loss, phase, mode_field, target):
    mode_count = mode_loss.shape[1]
    waves_here = phase.shape[1]
    devices = lax.axis_size("cell")
    place = lax.axis_index("cell")

    selected = jnp.take(interfaces, cell_section, axis=0)[:, None]
    amplitude = jnp.take(mode_loss, cell_profile, axis=0)[:, None, :]
    angle = jnp.take(phase, cell_profile, axis=0)
    cells = build_cells(selected, amplitude * jnp.cos(angle), amplitude * jnp.sin(angle))

    unit = jnp.stack(
        [jnp.eye(mode_count, dtype=jnp.float32), jnp.zeros((mode_count, mode_count), jnp.float32)]
    )
    unit = jnp.broadcast_to(unit, (waves_here, 2, mode_count, mode_count))
    zero = jnp.zeros_like(unit)

    local_suffix = suffix_scan(cells)
    prefix_input = cells[1]
    local_incoming = None
    block = jax.tree.map(lambda a: a[0], local_suffix)

    row_count = mode_count // devices
    total = block
    right = (zero, unit, unit)
    left = unit
    shift = 1
    while shift < devices // 2:
        perm = [(i, i ^ shift) for i in range(devices)]
        payload = jnp.stack(total)
        if local_incoming is None and shift > 1:
            payload, prefix_input = lax.optimization_barrier((payload, prefix_input))
            local_prefix = prefix_scan(prefix_input)
            local_incoming = jnp.concatenate([unit[None], local_prefix[:-1]], axis=0)
        other = exchange(payload, shift, devices, place)
        other = (other[0], other[1], other[2])
        upper = (place & shift) == 0
        first = pick(upper, total, other)
        second = pick(upper, other, total)
        total = star(first, second)
        right = pick(upper, star(right, other), right)
        left = jnp.where(upper, left, cmul(left, other[1]))
        shift *= 2

    perm = [(i, i ^ shift) for i in range(devices)]
    partner = place ^ shift
    pair = 2 if shift > 1 else 1
    rows_out = lax.dynamic_slice_in_dim(total[2], (partner - (partner % pair)) * row_count, pair * row_count, 2)
    sent = jnp.concatenate([total[0], total[1], rows_out], axis=2)
    got = exchange(sent, shift, devices, place)
    other_refl = got[:, :, :mode_count]
    other_trans = got[:, :, mode_count : 2 * mode_count]
    other_rows = lax.dynamic_slice_in_dim(got, 2 * mode_count + (place % pair) * row_count, row_count, 2)
    upper = (place & shift) == 0
    own_rows = lax.dynamic_slice_in_dim(total[2], place * row_count, row_count, 2)
    first_refl = jnp.where(upper, total[0], other_refl)
    first_trans = jnp.where(upper, total[1], other_trans)
    first_rows = jnp.where(upper, own_rows, other_rows)
    second_refl = jnp.where(upper, other_refl, total[0])
    second_trans = jnp.where(upper, other_trans, total[1])
    joined = star(
        (right[0], right[1], right[2]),
        (other_refl, other_trans, None),
        need_back=False,
    )
    right = (jnp.where(upper, joined[0], right[0]), jnp.where(upper, joined[1], right[1]))
    left = jnp.where(upper, left, cmul(left, other_trans))
    total_trans = cmul(second_trans, first_trans)
    mine = lax.dynamic_slice_in_dim(first_refl, place * row_count, row_count, 2) + cmul(
        cmul(first_rows, second_refl), first_trans
    )


    if local_incoming is None:
        local_prefix = prefix_scan(prefix_input)
        local_incoming = jnp.concatenate([unit[None], local_prefix[:-1]], axis=0)

    suffix_refl = local_suffix[0] + cmul(cmul(local_suffix[2], right[0][None]), local_suffix[1])
    suffix_trans = cmul(right[1][None], local_suffix[1])
    incoming = cmul(local_incoming, left[None])

    mismatch = total_trans - target
    fields = incoming + cmul(suffix_refl, incoming)
    adjoint = cmul(jnp.swapaxes(suffix_trans, -1, -2), mismatch[None])
    coupling = jnp.einsum(
        "cwij,cwkj->cik", fields[:, :, 0], adjoint[:, :, 0], precision=HIGHEST
    ) - jnp.einsum("cwij,cwkj->cik", fields[:, :, 1], adjoint[:, :, 1], precision=HIGHEST)
    summed = wl_sum(coupling)
    chosen = jnp.take(mode_field, cell_profile, axis=0)
    weighted = jnp.einsum("cmn,cnx->cmx", summed, chosen, precision=HIGHEST)
    gradient = jnp.sum(chosen * weighted, axis=1)

    return (mine, gradient)


def solution(mesh):
    in_specs = (
        P(),
        P("cell"),
        P("cell"),
        P(),
        P(None, "wl", None),
        P(None, None, "wl"),
        P("wl", None, None, None),
    )
    out_specs = (P("wl", None, "cell", None), P("cell", "wl"))
    return jax.shard_map(body, mesh=mesh, in_specs=in_specs, out_specs=out_specs, check_vma=False)
```

```python
import functools

import jax
import jax.numpy as jnp
from jax import lax
from jax.experimental import pallas as pl
from jax.experimental.pallas import tpu as pltpu
from jax.sharding import PartitionSpec as P

HIGHEST = lax.Precision.HIGHEST


def cmul(left, right):
    parts = jnp.einsum("...pmk,...qkn->...pqmn", left, right, precision=HIGHEST)
    real = parts[..., 0, 0, :, :] - parts[..., 1, 1, :, :]
    imag = parts[..., 0, 1, :, :] + parts[..., 1, 0, :, :]
    return jnp.stack([real, imag], axis=-3)


def star(former, latter, need_back=True):
    refl_f, trans_f, back_f = former
    refl_l, trans_l, back_l = latter
    reflect = refl_f + cmul(cmul(back_f, refl_l), trans_f)
    trans = cmul(trans_l, trans_f)
    back = cmul(back_f, back_l) if need_back else None
    return (reflect, trans, back)


def pick(flag, a, b):
    return jax.tree.map(lambda u, v: jnp.where(flag, u, v), a, b)


def cat(a, b):
    return jax.tree.map(lambda u, v: jnp.concatenate([u, v], axis=0), a, b)


def interleave(even, odd):
    return jnp.stack([even, odd], axis=1).reshape((-1,) + even.shape[1:])


def suffix_scan(cells):
    count = cells[0].shape[0]
    shift = 1
    while shift < count:
        head = jax.tree.map(lambda a: a[: count - shift], cells)
        tail = jax.tree.map(lambda a: a[shift:], cells)
        joined = star(head, tail)
        cells = cat(joined, jax.tree.map(lambda a: a[count - shift :], cells))
        shift *= 2
    return cells


def prefix_scan(trans):
    count = trans.shape[0]
    shift = 1
    while shift < count:
        joined = cmul(trans[shift:], trans[: count - shift])
        trans = jnp.concatenate([trans[:shift], joined], axis=0)
        shift *= 2
    return trans


def build_cells(selected, prop_real, prop_imag):
    forward = selected[:, :, 1]
    backward = selected[:, :, 2]
    row_real = prop_real[..., :, None]
    row_imag = prop_imag[..., :, None]
    trans = jnp.stack(
        [
            row_real * forward[:, :, 0] - row_imag * forward[:, :, 1],
            row_real * forward[:, :, 1] + row_imag * forward[:, :, 0],
        ],
        axis=2,
    )
    col_real = prop_real[..., None, :]
    col_imag = prop_imag[..., None, :]
    back = jnp.stack(
        [
            backward[:, :, 0] * col_real - backward[:, :, 1] * col_imag,
            backward[:, :, 0] * col_imag + backward[:, :, 1] * col_real,
        ],
        axis=2,
    )
    reflect = jnp.broadcast_to(selected[:, :, 0], trans.shape)
    return (reflect, trans, back)


def wl_sum_kernel(count, part_ref, out_ref, held, send_a, recv_a, send_b, recv_b):
    me = lax.axis_index("wl")
    row = lax.axis_index("cell")
    mesh_id = pl.DeviceIdType.MESH

    def link(src, dst, send, recv, peer):
        return pltpu.make_async_remote_copy(
            src_ref=src, dst_ref=dst, send_sem=send, recv_sem=recv,
            device_id=(peer, row), device_id_type=mesh_id,
        )

    barrier = pltpu.get_barrier_semaphore()
    for step in range(1, count):
        peer = lax.rem(me + step, count)
        pl.semaphore_signal(barrier, inc=1, device_id=(peer, row), device_id_type=mesh_id)
    pl.semaphore_wait(barrier, count - 1)

    outgoing = []
    for step in range(1, count):
        peer = lax.rem(me + step, count)
        copy = link(part_ref.at[peer], held.at[me], send_a.at[peer], recv_a.at[me], peer)
        copy.start()
        outgoing.append(copy)
    total = part_ref[me]
    for step in range(1, count):
        source = lax.rem(me + count - step, count)
        link(part_ref.at[source], held.at[source], send_a.at[source], recv_a.at[source], source).wait_recv()
        total = total + held[source]
    out_ref[me] = total
    for copy in outgoing:
        copy.wait_send()

    outgoing = []
    for step in range(1, count):
        peer = lax.rem(me + step, count)
        copy = link(out_ref.at[me], out_ref.at[me], send_b.at[peer], recv_b.at[me], peer)
        copy.start()
        outgoing.append(copy)
    for step in range(1, count):
        source = lax.rem(me + count - step, count)
        link(out_ref.at[source], out_ref.at[source], send_b.at[source], recv_b.at[source], source).wait_recv()
    for copy in outgoing:
        copy.wait_send()


def wl_sum(value):
    count = lax.axis_size("wl")
    lanes = value.shape[-1]
    parts = value.reshape(count, -1, lanes)
    summed = pl.pallas_call(
        functools.partial(wl_sum_kernel, count),
        out_shape=jax.ShapeDtypeStruct(parts.shape, parts.dtype),
        in_specs=[pl.BlockSpec(memory_space=pltpu.VMEM)],
        out_specs=pl.BlockSpec(memory_space=pltpu.VMEM),
        scratch_shapes=[
            pltpu.VMEM(parts.shape, parts.dtype),
            pltpu.SemaphoreType.DMA((count,)),
            pltpu.SemaphoreType.DMA((count,)),
            pltpu.SemaphoreType.DMA((count,)),
            pltpu.SemaphoreType.DMA((count,)),
        ],
        compiler_params=pltpu.CompilerParams(collective_id=0, has_side_effects=True),
    )(parts)
    return summed.reshape(value.shape)


def exchange(payload, shift, devices, place):
    perm = [(i, i ^ shift) for i in range(devices)]
    if shift == 1:
        return lax.ppermute(payload, "cell", perm)
    core = place & 1
    half = payload.shape[-2] // 2
    mine = lax.dynamic_slice_in_dim(payload, core * half, half, payload.ndim - 2)
    got = lax.ppermute(mine, "cell", perm)
    sibling = lax.ppermute(got, "cell", [(i, i ^ 1) for i in range(devices)])
    low = jnp.where(core == 0, got, sibling)
    high = jnp.where(core == 0, sibling, got)
    return jnp.concatenate([low, high], axis=payload.ndim - 2)


def body(interfaces, cell_profile, cell_section, mode_loss, phase, mode_field, target):
    mode_count = mode_loss.shape[1]
    waves_here = phase.shape[1]
    devices = lax.axis_size("cell")
    place = lax.axis_index("cell")

    selected = jnp.take(interfaces, cell_section, axis=0)[:, None]
    amplitude = jnp.take(mode_loss, cell_profile, axis=0)[:, None, :]
    angle = jnp.take(phase, cell_profile, axis=0)
    cells = build_cells(selected, amplitude * jnp.cos(angle), amplitude * jnp.sin(angle))

    unit = jnp.stack(
        [jnp.eye(mode_count, dtype=jnp.float32), jnp.zeros((mode_count, mode_count), jnp.float32)]
    )
    unit = jnp.broadcast_to(unit, (waves_here, 2, mode_count, mode_count))
    zero = jnp.zeros_like(unit)

    local_suffix = suffix_scan(cells)
    prefix_input = cells[1]
    local_incoming = None
    block = jax.tree.map(lambda a: a[0], local_suffix)

    row_count = mode_count // devices
    total = block
    right = (zero, unit, unit)
    left = unit
    shift = 1
    while shift < devices // 2:
        perm = [(i, i ^ shift) for i in range(devices)]
        payload = jnp.stack(total)
        if local_incoming is None and shift > 1:
            payload, prefix_input = lax.optimization_barrier((payload, prefix_input))
            local_prefix = prefix_scan(prefix_input)
            local_incoming = jnp.concatenate([unit[None], local_prefix[:-1]], axis=0)
        other = exchange(payload, shift, devices, place)
        other = (other[0], other[1], other[2])
        upper = (place & shift) == 0
        first = pick(upper, total, other)
        second = pick(upper, other, total)
        joined = star(
            jax.tree.map(lambda a, b: jnp.stack([a, b]), right, first),
            jax.tree.map(lambda a, b: jnp.stack([a, b]), other, second),
        )
        right = pick(upper, jax.tree.map(lambda a: a[0], joined), right)
        total = jax.tree.map(lambda a: a[1], joined)
        left = jnp.where(upper, left, cmul(left, other[1]))
        shift *= 2

    perm = [(i, i ^ shift) for i in range(devices)]
    partner = place ^ shift
    pair = 2 if shift > 1 else 1
    rows_out = lax.dynamic_slice_in_dim(total[2], (partner - (partner % pair)) * row_count, pair * row_count, 2)
    sent = jnp.concatenate([total[0], total[1], rows_out], axis=2)
    got = exchange(sent, shift, devices, place)
    other_refl = got[:, :, :mode_count]
    other_trans = got[:, :, mode_count : 2 * mode_count]
    other_rows = lax.dynamic_slice_in_dim(got, 2 * mode_count + (place % pair) * row_count, row_count, 2)
    upper = (place & shift) == 0
    own_rows = lax.dynamic_slice_in_dim(total[2], place * row_count, row_count, 2)
    first_refl = jnp.where(upper, total[0], other_refl)
    first_trans = jnp.where(upper, total[1], other_trans)
    first_rows = jnp.where(upper, own_rows, other_rows)
    second_refl = jnp.where(upper, other_refl, total[0])
    second_trans = jnp.where(upper, other_trans, total[1])
    joined = star(
        (right[0], right[1], right[2]),
        (other_refl, other_trans, None),
        need_back=False,
    )
    right = (jnp.where(upper, joined[0], right[0]), jnp.where(upper, joined[1], right[1]))
    left = jnp.where(upper, left, cmul(left, other_trans))
    total_trans = cmul(second_trans, first_trans)
    mine = lax.dynamic_slice_in_dim(first_refl, place * row_count, row_count, 2) + cmul(
        cmul(first_rows, second_refl), first_trans
    )


    if local_incoming is None:
        local_prefix = prefix_scan(prefix_input)
        local_incoming = jnp.concatenate([unit[None], local_prefix[:-1]], axis=0)

    suffix_refl = local_suffix[0] + cmul(cmul(local_suffix[2], right[0][None]), local_suffix[1])
    suffix_trans = cmul(right[1][None], local_suffix[1])
    incoming = cmul(local_incoming, left[None])

    mismatch = total_trans - target
    fields = incoming + cmul(suffix_refl, incoming)
    adjoint = cmul(jnp.swapaxes(suffix_trans, -1, -2), mismatch[None])
    coupling = jnp.einsum(
        "cwij,cwkj->cik", fields[:, :, 0], adjoint[:, :, 0], precision=lax.Precision.HIGH
    ) - jnp.einsum("cwij,cwkj->cik", fields[:, :, 1], adjoint[:, :, 1], precision=lax.Precision.HIGH)
    summed = wl_sum(coupling)
    chosen = jnp.take(mode_field, cell_profile, axis=0)
    weighted = jnp.einsum("cmn,cnx->cmx", summed, chosen, precision=lax.Precision.HIGH)
    gradient = jnp.sum(chosen * weighted, axis=1)

    return (mine, gradient)


def solution(mesh):
    in_specs = (
        P(),
        P("cell"),
        P("cell"),
        P(),
        P(None, "wl", None),
        P(None, None, "wl"),
        P("wl", None, None, None),
    )
    out_specs = (P("wl", None, "cell", None), P("cell", "wl"))
    return jax.shard_map(body, mesh=mesh, in_specs=in_specs, out_specs=out_specs, check_vma=False)
```

```python
import functools

import jax
import jax.numpy as jnp
from jax import lax
from jax.experimental import pallas as pl
from jax.experimental.pallas import tpu as pltpu
from jax.sharding import PartitionSpec as P

HIGHEST = lax.Precision.HIGHEST


def cmul(left, right, precision=HIGHEST):
    parts = jnp.einsum("...pmk,...qkn->...pqmn", left, right, precision=precision)
    real = parts[..., 0, 0, :, :] - parts[..., 1, 1, :, :]
    imag = parts[..., 0, 1, :, :] + parts[..., 1, 0, :, :]
    return jnp.stack([real, imag], axis=-3)


def star(former, latter, need_back=True):
    refl_f, trans_f, back_f = former
    refl_l, trans_l, back_l = latter
    reflect = refl_f + cmul(cmul(back_f, refl_l), trans_f)
    trans = cmul(trans_l, trans_f)
    back = cmul(back_f, back_l) if need_back else None
    return (reflect, trans, back)


def pick(flag, a, b):
    return jax.tree.map(lambda u, v: jnp.where(flag, u, v), a, b)


def cat(a, b):
    return jax.tree.map(lambda u, v: jnp.concatenate([u, v], axis=0), a, b)


def interleave(even, odd):
    return jnp.stack([even, odd], axis=1).reshape((-1,) + even.shape[1:])


def suffix_scan(cells):
    count = cells[0].shape[0]
    shift = 1
    while shift < count:
        head = jax.tree.map(lambda a: a[: count - shift], cells)
        tail = jax.tree.map(lambda a: a[shift:], cells)
        joined = star(head, tail)
        cells = cat(joined, jax.tree.map(lambda a: a[count - shift :], cells))
        shift *= 2
    return cells


def prefix_scan(trans):
    count = trans.shape[0]
    shift = 1
    while shift < count:
        joined = cmul(trans[shift:], trans[: count - shift])
        trans = jnp.concatenate([trans[:shift], joined], axis=0)
        shift *= 2
    return trans


def build_cells(selected, prop_real, prop_imag):
    forward = selected[:, :, 1]
    backward = selected[:, :, 2]
    row_real = prop_real[..., :, None]
    row_imag = prop_imag[..., :, None]
    trans = jnp.stack(
        [
            row_real * forward[:, :, 0] - row_imag * forward[:, :, 1],
            row_real * forward[:, :, 1] + row_imag * forward[:, :, 0],
        ],
        axis=2,
    )
    col_real = prop_real[..., None, :]
    col_imag = prop_imag[..., None, :]
    back = jnp.stack(
        [
            backward[:, :, 0] * col_real - backward[:, :, 1] * col_imag,
            backward[:, :, 0] * col_imag + backward[:, :, 1] * col_real,
        ],
        axis=2,
    )
    reflect = jnp.broadcast_to(selected[:, :, 0], trans.shape)
    return (reflect, trans, back)


def wl_sum_kernel(count, part_ref, out_ref, held, send_a, recv_a, send_b, recv_b):
    me = lax.axis_index("wl")
    row = lax.axis_index("cell")
    mesh_id = pl.DeviceIdType.MESH

    def link(src, dst, send, recv, peer):
        return pltpu.make_async_remote_copy(
            src_ref=src, dst_ref=dst, send_sem=send, recv_sem=recv,
            device_id=(peer, row), device_id_type=mesh_id,
        )

    barrier = pltpu.get_barrier_semaphore()
    for step in range(1, count):
        peer = lax.rem(me + step, count)
        pl.semaphore_signal(barrier, inc=1, device_id=(peer, row), device_id_type=mesh_id)
    pl.semaphore_wait(barrier, count - 1)

    outgoing = []
    for step in range(1, count):
        peer = lax.rem(me + step, count)
        copy = link(part_ref.at[peer], held.at[me], send_a.at[peer], recv_a.at[me], peer)
        copy.start()
        outgoing.append(copy)
    total = part_ref[me]
    for step in range(1, count):
        source = lax.rem(me + count - step, count)
        link(part_ref.at[source], held.at[source], send_a.at[source], recv_a.at[source], source).wait_recv()
        total = total + held[source]
    out_ref[me] = total
    for copy in outgoing:
        copy.wait_send()

    outgoing = []
    for step in range(1, count):
        peer = lax.rem(me + step, count)
        copy = link(out_ref.at[me], out_ref.at[me], send_b.at[peer], recv_b.at[me], peer)
        copy.start()
        outgoing.append(copy)
    for step in range(1, count):
        source = lax.rem(me + count - step, count)
        link(out_ref.at[source], out_ref.at[source], send_b.at[source], recv_b.at[source], source).wait_recv()
    for copy in outgoing:
        copy.wait_send()


def wl_sum(value):
    count = lax.axis_size("wl")
    lanes = value.shape[-1]
    parts = value.reshape(count, -1, lanes)
    summed = pl.pallas_call(
        functools.partial(wl_sum_kernel, count),
        out_shape=jax.ShapeDtypeStruct(parts.shape, parts.dtype),
        in_specs=[pl.BlockSpec(memory_space=pltpu.VMEM)],
        out_specs=pl.BlockSpec(memory_space=pltpu.VMEM),
        scratch_shapes=[
            pltpu.VMEM(parts.shape, parts.dtype),
            pltpu.SemaphoreType.DMA((count,)),
            pltpu.SemaphoreType.DMA((count,)),
            pltpu.SemaphoreType.DMA((count,)),
            pltpu.SemaphoreType.DMA((count,)),
        ],
        compiler_params=pltpu.CompilerParams(collective_id=0, has_side_effects=True),
    )(parts)
    return summed.reshape(value.shape)


def exchange(payload, shift, devices, place):
    perm = [(i, i ^ shift) for i in range(devices)]
    if shift == 1:
        return lax.ppermute(payload, "cell", perm)
    core = place & 1
    half = payload.shape[-2] // 2
    mine = lax.dynamic_slice_in_dim(payload, core * half, half, payload.ndim - 2)
    got = lax.ppermute(mine, "cell", perm)
    sibling = lax.ppermute(got, "cell", [(i, i ^ 1) for i in range(devices)])
    low = jnp.where(core == 0, got, sibling)
    high = jnp.where(core == 0, sibling, got)
    return jnp.concatenate([low, high], axis=payload.ndim - 2)


def body(interfaces, cell_profile, cell_section, mode_loss, phase, mode_field, target):
    mode_count = mode_loss.shape[1]
    waves_here = phase.shape[1]
    devices = lax.axis_size("cell")
    place = lax.axis_index("cell")

    selected = jnp.take(interfaces, cell_section, axis=0)[:, None]
    amplitude = jnp.take(mode_loss, cell_profile, axis=0)[:, None, :]
    angle = jnp.take(phase, cell_profile, axis=0)
    cells = build_cells(selected, amplitude * jnp.cos(angle), amplitude * jnp.sin(angle))

    unit = jnp.stack(
        [jnp.eye(mode_count, dtype=jnp.float32), jnp.zeros((mode_count, mode_count), jnp.float32)]
    )
    unit = jnp.broadcast_to(unit, (waves_here, 2, mode_count, mode_count))
    zero = jnp.zeros_like(unit)

    local_suffix = suffix_scan(cells)
    prefix_input = cells[1]
    local_incoming = None
    block = jax.tree.map(lambda a: a[0], local_suffix)

    row_count = mode_count // devices
    total = block
    right = (zero, unit, unit)
    left = unit
    shift = 1
    while shift < devices // 2:
        perm = [(i, i ^ shift) for i in range(devices)]
        payload = jnp.stack(total)
        if local_incoming is None and shift > 1:
            payload, prefix_input = lax.optimization_barrier((payload, prefix_input))
            local_prefix = prefix_scan(prefix_input)
            local_incoming = jnp.concatenate([unit[None], local_prefix[:-1]], axis=0)
        other = exchange(payload, shift, devices, place)
        other = (other[0], other[1], other[2])
        upper = (place & shift) == 0
        first = pick(upper, total, other)
        second = pick(upper, other, total)
        joined = star(
            jax.tree.map(lambda a, b: jnp.stack([a, b]), right, first),
            jax.tree.map(lambda a, b: jnp.stack([a, b]), other, second),
        )
        right = pick(upper, jax.tree.map(lambda a: a[0], joined), right)
        total = jax.tree.map(lambda a: a[1], joined)
        left = jnp.where(upper, left, cmul(left, other[1]))
        shift *= 2

    perm = [(i, i ^ shift) for i in range(devices)]
    partner = place ^ shift
    pair = 2 if shift > 1 else 1
    rows_out = lax.dynamic_slice_in_dim(total[2], (partner - (partner % pair)) * row_count, pair * row_count, 2)
    sent = jnp.concatenate([total[0], total[1], rows_out], axis=2)
    got = exchange(sent, shift, devices, place)
    other_refl = got[:, :, :mode_count]
    other_trans = got[:, :, mode_count : 2 * mode_count]
    other_rows = lax.dynamic_slice_in_dim(got, 2 * mode_count + (place % pair) * row_count, row_count, 2)
    upper = (place & shift) == 0
    own_rows = lax.dynamic_slice_in_dim(total[2], place * row_count, row_count, 2)
    first_refl = jnp.where(upper, total[0], other_refl)
    first_trans = jnp.where(upper, total[1], other_trans)
    first_rows = jnp.where(upper, own_rows, other_rows)
    second_refl = jnp.where(upper, other_refl, total[0])
    second_trans = jnp.where(upper, other_trans, total[1])
    joined = star(
        (right[0], right[1], right[2]),
        (other_refl, other_trans, None),
        need_back=False,
    )
    right = (jnp.where(upper, joined[0], right[0]), jnp.where(upper, joined[1], right[1]))
    left = jnp.where(upper, left, cmul(left, other_trans))
    total_trans = cmul(second_trans, first_trans)
    mine = lax.dynamic_slice_in_dim(first_refl, place * row_count, row_count, 2) + cmul(
        cmul(first_rows, second_refl), first_trans
    )


    if local_incoming is None:
        local_prefix = prefix_scan(prefix_input)
        local_incoming = jnp.concatenate([unit[None], local_prefix[:-1]], axis=0)

    high = lax.Precision.HIGH
    suffix_refl = local_suffix[0] + cmul(cmul(local_suffix[2], right[0][None], high), local_suffix[1], high)
    suffix_trans = cmul(right[1][None], local_suffix[1], high)
    incoming = cmul(local_incoming, left[None], high)

    mismatch = total_trans - target
    fields = incoming + cmul(suffix_refl, incoming, high)
    adjoint = cmul(jnp.swapaxes(suffix_trans, -1, -2), mismatch[None], high)
    coupling = jnp.einsum(
        "cwij,cwkj->cik", fields[:, :, 0], adjoint[:, :, 0], precision=lax.Precision.HIGH
    ) - jnp.einsum("cwij,cwkj->cik", fields[:, :, 1], adjoint[:, :, 1], precision=lax.Precision.HIGH)
    summed = wl_sum(coupling)
    chosen = jnp.take(mode_field, cell_profile, axis=0)
    weighted = jnp.einsum("cmn,cnx->cmx", summed, chosen, precision=lax.Precision.HIGH)
    gradient = jnp.sum(chosen * weighted, axis=1)

    return (mine, gradient)


def solution(mesh):
    in_specs = (
        P(),
        P("cell"),
        P("cell"),
        P(),
        P(None, "wl", None),
        P(None, None, "wl"),
        P("wl", None, None, None),
    )
    out_specs = (P("wl", None, "cell", None), P("cell", "wl"))
    return jax.shard_map(body, mesh=mesh, in_specs=in_specs, out_specs=out_specs, check_vma=False)
```

```python
import functools

import jax
import jax.numpy as jnp
from jax import lax
from jax.experimental import pallas as pl
from jax.experimental.pallas import tpu as pltpu
from jax.sharding import PartitionSpec as P

HIGHEST = lax.Precision.HIGHEST


def cmul(left, right, precision=HIGHEST):
    parts = jnp.einsum("...pmk,...qkn->...pqmn", left, right, precision=precision)
    real = parts[..., 0, 0, :, :] - parts[..., 1, 1, :, :]
    imag = parts[..., 0, 1, :, :] + parts[..., 1, 0, :, :]
    return jnp.stack([real, imag], axis=-3)


def star(former, latter, need_back=True, precision=HIGHEST):
    refl_f, trans_f, back_f = former
    refl_l, trans_l, back_l = latter
    reflect = refl_f + cmul(cmul(back_f, refl_l, precision), trans_f, precision)
    trans = cmul(trans_l, trans_f, precision)
    back = cmul(back_f, back_l, precision) if need_back else None
    return (reflect, trans, back)


def pick(flag, a, b):
    return jax.tree.map(lambda u, v: jnp.where(flag, u, v), a, b)


def cat(a, b):
    return jax.tree.map(lambda u, v: jnp.concatenate([u, v], axis=0), a, b)


def interleave(even, odd):
    return jnp.stack([even, odd], axis=1).reshape((-1,) + even.shape[1:])


def suffix_scan(cells):
    count = cells[0].shape[0]
    shift = 1
    while shift < count:
        head = jax.tree.map(lambda a: a[: count - shift], cells)
        tail = jax.tree.map(lambda a: a[shift:], cells)
        joined = star(head, tail)
        cells = cat(joined, jax.tree.map(lambda a: a[count - shift :], cells))
        shift *= 2
    return cells


def prefix_scan(trans):
    count = trans.shape[0]
    shift = 1
    while shift < count:
        joined = cmul(trans[shift:], trans[: count - shift])
        trans = jnp.concatenate([trans[:shift], joined], axis=0)
        shift *= 2
    return trans


def build_cells(selected, prop_real, prop_imag):
    forward = selected[:, :, 1]
    backward = selected[:, :, 2]
    row_real = prop_real[..., :, None]
    row_imag = prop_imag[..., :, None]
    trans = jnp.stack(
        [
            row_real * forward[:, :, 0] - row_imag * forward[:, :, 1],
            row_real * forward[:, :, 1] + row_imag * forward[:, :, 0],
        ],
        axis=2,
    )
    col_real = prop_real[..., None, :]
    col_imag = prop_imag[..., None, :]
    back = jnp.stack(
        [
            backward[:, :, 0] * col_real - backward[:, :, 1] * col_imag,
            backward[:, :, 0] * col_imag + backward[:, :, 1] * col_real,
        ],
        axis=2,
    )
    reflect = jnp.broadcast_to(selected[:, :, 0], trans.shape)
    return (reflect, trans, back)


def wl_sum_kernel(count, part_ref, out_ref, held, send_a, recv_a, send_b, recv_b):
    me = lax.axis_index("wl")
    row = lax.axis_index("cell")
    mesh_id = pl.DeviceIdType.MESH

    def link(src, dst, send, recv, peer):
        return pltpu.make_async_remote_copy(
            src_ref=src, dst_ref=dst, send_sem=send, recv_sem=recv,
            device_id=(peer, row), device_id_type=mesh_id,
        )

    barrier = pltpu.get_barrier_semaphore()
    for step in range(1, count):
        peer = lax.rem(me + step, count)
        pl.semaphore_signal(barrier, inc=1, device_id=(peer, row), device_id_type=mesh_id)
    pl.semaphore_wait(barrier, count - 1)

    outgoing = []
    for step in range(1, count):
        peer = lax.rem(me + step, count)
        copy = link(part_ref.at[peer], held.at[me], send_a.at[peer], recv_a.at[me], peer)
        copy.start()
        outgoing.append(copy)
    total = part_ref[me]
    for step in range(1, count):
        source = lax.rem(me + count - step, count)
        link(part_ref.at[source], held.at[source], send_a.at[source], recv_a.at[source], source).wait_recv()
        total = total + held[source]
    out_ref[me] = total
    for copy in outgoing:
        copy.wait_send()

    outgoing = []
    for step in range(1, count):
        peer = lax.rem(me + step, count)
        copy = link(out_ref.at[me], out_ref.at[me], send_b.at[peer], recv_b.at[me], peer)
        copy.start()
        outgoing.append(copy)
    for step in range(1, count):
        source = lax.rem(me + count - step, count)
        link(out_ref.at[source], out_ref.at[source], send_b.at[source], recv_b.at[source], source).wait_recv()
    for copy in outgoing:
        copy.wait_send()


def wl_sum(value):
    count = lax.axis_size("wl")
    lanes = value.shape[-1]
    parts = value.reshape(count, -1, lanes)
    summed = pl.pallas_call(
        functools.partial(wl_sum_kernel, count),
        out_shape=jax.ShapeDtypeStruct(parts.shape, parts.dtype),
        in_specs=[pl.BlockSpec(memory_space=pltpu.VMEM)],
        out_specs=pl.BlockSpec(memory_space=pltpu.VMEM),
        scratch_shapes=[
            pltpu.VMEM(parts.shape, parts.dtype),
            pltpu.SemaphoreType.DMA((count,)),
            pltpu.SemaphoreType.DMA((count,)),
            pltpu.SemaphoreType.DMA((count,)),
            pltpu.SemaphoreType.DMA((count,)),
        ],
        compiler_params=pltpu.CompilerParams(collective_id=0, has_side_effects=True),
    )(parts)
    return summed.reshape(value.shape)


def exchange(payload, shift, devices, place):
    perm = [(i, i ^ shift) for i in range(devices)]
    if shift == 1:
        return lax.ppermute(payload, "cell", perm)
    core = place & 1
    half = payload.shape[-2] // 2
    mine = lax.dynamic_slice_in_dim(payload, core * half, half, payload.ndim - 2)
    got = lax.ppermute(mine, "cell", perm)
    sibling = lax.ppermute(got, "cell", [(i, i ^ 1) for i in range(devices)])
    low = jnp.where(core == 0, got, sibling)
    high = jnp.where(core == 0, sibling, got)
    return jnp.concatenate([low, high], axis=payload.ndim - 2)


def body(interfaces, cell_profile, cell_section, mode_loss, phase, mode_field, target):
    mode_count = mode_loss.shape[1]
    waves_here = phase.shape[1]
    devices = lax.axis_size("cell")
    place = lax.axis_index("cell")

    selected = jnp.take(interfaces, cell_section, axis=0)[:, None]
    amplitude = jnp.take(mode_loss, cell_profile, axis=0)[:, None, :]
    angle = jnp.take(phase, cell_profile, axis=0)
    cells = build_cells(selected, amplitude * jnp.cos(angle), amplitude * jnp.sin(angle))

    unit = jnp.stack(
        [jnp.eye(mode_count, dtype=jnp.float32), jnp.zeros((mode_count, mode_count), jnp.float32)]
    )
    unit = jnp.broadcast_to(unit, (waves_here, 2, mode_count, mode_count))
    zero = jnp.zeros_like(unit)

    local_suffix = suffix_scan(cells)
    prefix_input = cells[1]
    local_incoming = None
    block = jax.tree.map(lambda a: a[0], local_suffix)

    row_count = mode_count // devices
    total = block
    right = (zero, unit, unit)
    left = unit
    shift = 1
    while shift < devices // 2:
        perm = [(i, i ^ shift) for i in range(devices)]
        payload = jnp.stack(total)
        if local_incoming is None and shift > 1:
            payload, prefix_input = lax.optimization_barrier((payload, prefix_input))
            local_prefix = prefix_scan(prefix_input)
            local_incoming = jnp.concatenate([unit[None], local_prefix[:-1]], axis=0)
        other = exchange(payload, shift, devices, place)
        other = (other[0], other[1], other[2])
        upper = (place & shift) == 0
        first = pick(upper, total, other)
        second = pick(upper, other, total)
        joined = star(
            jax.tree.map(lambda a, b: jnp.stack([a, b]), right, first),
            jax.tree.map(lambda a, b: jnp.stack([a, b]), other, second),
            precision=lax.Precision.HIGH,
        )
        right = pick(upper, jax.tree.map(lambda a: a[0], joined), right)
        total = jax.tree.map(lambda a: a[1], joined)
        left = jnp.where(upper, left, cmul(left, other[1]))
        shift *= 2

    perm = [(i, i ^ shift) for i in range(devices)]
    partner = place ^ shift
    pair = 2 if shift > 1 else 1
    rows_out = lax.dynamic_slice_in_dim(total[2], (partner - (partner % pair)) * row_count, pair * row_count, 2)
    sent = jnp.concatenate([total[0], total[1], rows_out], axis=2)
    got = exchange(sent, shift, devices, place)
    other_refl = got[:, :, :mode_count]
    other_trans = got[:, :, mode_count : 2 * mode_count]
    other_rows = lax.dynamic_slice_in_dim(got, 2 * mode_count + (place % pair) * row_count, row_count, 2)
    upper = (place & shift) == 0
    own_rows = lax.dynamic_slice_in_dim(total[2], place * row_count, row_count, 2)
    first_refl = jnp.where(upper, total[0], other_refl)
    first_trans = jnp.where(upper, total[1], other_trans)
    first_rows = jnp.where(upper, own_rows, other_rows)
    second_refl = jnp.where(upper, other_refl, total[0])
    second_trans = jnp.where(upper, other_trans, total[1])
    joined = star(
        (right[0], right[1], right[2]),
        (other_refl, other_trans, None),
        need_back=False,
    )
    right = (jnp.where(upper, joined[0], right[0]), jnp.where(upper, joined[1], right[1]))
    left = jnp.where(upper, left, cmul(left, other_trans))
    total_trans = cmul(second_trans, first_trans)
    mine = lax.dynamic_slice_in_dim(first_refl, place * row_count, row_count, 2) + cmul(
        cmul(first_rows, second_refl), first_trans
    )


    if local_incoming is None:
        local_prefix = prefix_scan(prefix_input)
        local_incoming = jnp.concatenate([unit[None], local_prefix[:-1]], axis=0)

    high = lax.Precision.HIGH
    suffix_refl = local_suffix[0] + cmul(cmul(local_suffix[2], right[0][None], high), local_suffix[1], high)
    suffix_trans = cmul(right[1][None], local_suffix[1], high)
    incoming = cmul(local_incoming, left[None], high)

    mismatch = total_trans - target
    fields = incoming + cmul(suffix_refl, incoming, high)
    adjoint = cmul(jnp.swapaxes(suffix_trans, -1, -2), mismatch[None], high)
    coupling = jnp.einsum(
        "cwij,cwkj->cik", fields[:, :, 0], adjoint[:, :, 0], precision=lax.Precision.HIGH
    ) - jnp.einsum("cwij,cwkj->cik", fields[:, :, 1], adjoint[:, :, 1], precision=lax.Precision.HIGH)
    summed = wl_sum(coupling)
    chosen = jnp.take(mode_field, cell_profile, axis=0)
    weighted = jnp.einsum("cmn,cnx->cmx", summed, chosen, precision=lax.Precision.HIGH)
    gradient = jnp.sum(chosen * weighted, axis=1)

    return (mine, gradient)


def solution(mesh):
    in_specs = (
        P(),
        P("cell"),
        P("cell"),
        P(),
        P(None, "wl", None),
        P(None, None, "wl"),
        P("wl", None, None, None),
    )
    out_specs = (P("wl", None, "cell", None), P("cell", "wl"))
    return jax.shard_map(body, mesh=mesh, in_specs=in_specs, out_specs=out_specs, check_vma=False)
```
